32 devices in a mesh: kv: 2 (over y), ctx: 16 (over z, x, core).
Axes of the slice: x: 2, y: 2, z: 4, core: 2. Of those that a mesh axis runs over, the one named last changes fastest.
Arguments:
- residual: bfloat16 [64, 8192], P(None, 'ctx'), may hold values from -8 to 8
- queries: bfloat16 [64, 8192], P(None, 'kv'), may hold values from -16 to 16
- draft_token_keys: bfloat16 [64, 1024], P(None, 'kv'), may hold values from -32 to 32
- draft_token_values: bfloat16 [64, 1024], P(None, 'kv'), may hold values from -8 to 8
- cache_keys: bfloat16 [2, 8192, 1024], P(None, 'ctx', 'kv'), may hold values from -32 to 32
- cached_value_rows: bfloat16 [2, 8192, 1024], P(None, 'ctx', 'kv'), may hold values from -8 to 8
- tenant_ids: int32 [64], replicated, may hold values from 0 to 1, as said below
- tree_mask: int32 [64, 64], replicated, may hold values from 0 to 1, as said below
- cache_lengths: int32 [2], replicated, may hold values from 4097 to 8192
- out_weight: bfloat16 [8192, 8192], P('kv', 'ctx'), may hold values from -0.0625 to 0.0625
- out_signs: bfloat16 [2, 8192, 8192], P(None, 'kv', 'ctx'), may hold values from -1 to 1, as said below
- norm_gain: float32 [8192], P('ctx'), may hold values from 0.1 to 1.9
- gate_weight: bfloat16 [8192, 16384], P(None, ('kv', 'ctx')), may hold values from -0.0625 to 0.0625
- up_weight: bfloat16 [8192, 16384], P(None, ('kv', 'ctx')), may hold values from -0.0625 to 0.0625
- down_weight: bfloat16 [16384, 8192], P(('kv', 'ctx')), may hold values from -0.09375 to 0.09375
- gate_signs: bfloat16 [2, 8192, 16384], P(None, None, ('kv', 'ctx')), may hold values from -1 to 1, as said below
- up_signs: bfloat16 [2, 8192, 16384], P(None, None, ('kv', 'ctx')), may hold values from -1 to 1, as said below
- down_signs: bfloat16 [2, 16384, 8192], P(None, ('kv', 'ctx')), may hold values from -1 to 1, as said below
- delta_scale: float32 [2, 4], replicated, may hold values from 0.3 to 0.9
Outputs:
- mixed: bfloat16 [64, 8192], P(None, 'ctx')
The draws below stay inside these ranges and needn't reach their ends.
Inputs may be any that keep to these rules, and one draw needn't show every extreme that they name: `tenant_ids`: exactly 32 tokens belong to each tenant. `tree_mask`: entry (i, j) is 1 exactly when token j is token i or an ancestor of token i in the draft tree of their common tenant; each tenant's 32 tokens form one tree. `out_signs`: every entry is 1 or -1. `gate_signs`: every entry is 1 or -1. `up_signs`: every entry is 1 or -1. `down_signs`: every entry is 1 or -1.
All inputs are finite; a program needn't handle non-finite values.
Results may differ from the reference program's by a relative error of at most 0.013.
Values may be sent and summed in bfloat16 or wider, within the bound.
No kernel may reach another device: no remote copies, remote signals or barrier semaphores. Data moves between devices by JAX's collectives and lax.ppermute only.
A program may use at most 192 MiB of HBM per device.

```python
import math
import jax
import jax.numpy as jnp
from jax import lax

D = 8192
QUERY_HEADS = 64
KEY_VALUE_HEADS = 8
HEAD_SIZE = 128
FF = 16384
TENANT_COUNT = 2
DRAFT_TOKENS = 32
ALL_TOKENS = 64
CACHE_SLOTS = 8192


def tree_parts(key):
    base_matrix = jax.random.fold_in(key, 7001)
    key_perm, key_parent = jax.random.split(base_matrix)
    shuffled = jax.random.permutation(key_perm, ALL_TOKENS).astype(jnp.int32)
    tenant_index = (shuffled // DRAFT_TOKENS).astype(jnp.int32)
    ranking = (shuffled % DRAFT_TOKENS).astype(jnp.int32)
    ranks = jnp.arange(DRAFT_TOKENS, dtype=jnp.int32)
    parent = jax.random.randint(key_parent, (TENANT_COUNT, DRAFT_TOKENS), 0, jnp.maximum(ranks, 1))
    parent_links = ((parent[:, :, None] == ranks[None, None, :]) & (ranks[None, :, None] > 0)).astype(jnp.int32)
    identity_matrix = jnp.broadcast_to(jnp.eye(DRAFT_TOKENS, dtype=jnp.int32), (TENANT_COUNT, DRAFT_TOKENS, DRAFT_TOKENS))

    def extend(step, reachable):
        return jnp.minimum(identity_matrix + jnp.einsum('dnv,dvo->dno', parent_links, reachable), 1)
    reachable = lax.fori_loop(0, DRAFT_TOKENS, extend, identity_matrix)
    same_tenant = (tenant_index[:, None] == tenant_index[None, :]).astype(jnp.int32)
    ancestry = reachable[tenant_index[:, None], ranking[:, None], ranking[None, :]] * same_tenant
    return (tenant_index, ancestry.astype(jnp.int32))


def draw_tenant_ids(key, part):
    return tree_parts(key)[0]


def draw_tree_mask(key, part):
    return tree_parts(key)[1]


def jitter_sample(key, shape):
    return jnp.clip(jax.random.normal(key, shape, jnp.float32), -4.0, 4.0)


def query_parts(key):
    base_matrix = jax.random.fold_in(key, 7002)
    key_common, key_own, key_jitter = jax.random.split(base_matrix, 3)
    tenant_index = tree_parts(key)[0]
    group_width = QUERY_HEADS // KEY_VALUE_HEADS
    common = jitter_sample(key_common, (TENANT_COUNT, QUERY_HEADS, HEAD_SIZE))
    own = jitter_sample(key_own, (ALL_TOKENS, QUERY_HEADS, HEAD_SIZE))
    additional = jitter_sample(key_jitter, (ALL_TOKENS, KEY_VALUE_HEADS, HEAD_SIZE))
    shared_part = common[tenant_index]
    query_matrix = 2.5 * (0.7 * shared_part + 0.71 * own)
    draft_key_matrix = 0.32 * 1.75 * shared_part.reshape(ALL_TOKENS, KEY_VALUE_HEADS, group_width, HEAD_SIZE).sum(axis=2) + 0.3 * additional
    return (query_matrix.reshape(ALL_TOKENS, QUERY_HEADS * HEAD_SIZE), draft_key_matrix.reshape(ALL_TOKENS, KEY_VALUE_HEADS * HEAD_SIZE))


def draw_queries(key, part):
    return query_parts(key)[0].astype(jnp.bfloat16)


def draw_draft_token_keys(key, part):
    return query_parts(key)[1].astype(jnp.bfloat16)


def draw_cache_keys(key, part):
    base_matrix = jax.random.fold_in(key, 7004)
    tenant_cache = jitter_sample(base_matrix, (TENANT_COUNT, CACHE_SLOTS, KEY_VALUE_HEADS * HEAD_SIZE))
    return tenant_cache.astype(jnp.bfloat16)


def draw_residual(key, part):
    base_matrix = jax.random.fold_in(key, 7005)
    ramp = jnp.arange(D, dtype=jnp.float32) / D
    values = jnp.clip(jax.random.normal(base_matrix, (ALL_TOKENS, D), jnp.float32), -4.0, 4.0) * (0.6 + 1.2 * ramp)
    return values.astype(jnp.bfloat16)


def sign_draw(key, salt, shape):
    flips = jax.random.bernoulli(jax.random.fold_in(key, salt), 0.5, shape)
    return jnp.where(flips, 1.0, -1.0).astype(jnp.float32).astype(jnp.bfloat16)


def draw_out_signs(key, part):
    return sign_draw(key, 7011, (TENANT_COUNT, QUERY_HEADS * HEAD_SIZE, D))


def draw_gate_signs(key, part):
    return sign_draw(key, 7012, (TENANT_COUNT, D, FF))


def draw_up_signs(key, part):
    return sign_draw(key, 7013, (TENANT_COUNT, D, FF))


def draw_down_signs(key, part):
    return sign_draw(key, 7014, (TENANT_COUNT, FF, D))


def with_spikes(values, own_key, source, target, shards_of, factor):
    def block_of(position):
        return (jnp.arange(values.shape[position]) // (values.shape[position] // shards_of)).reshape((-1,) + (1,) * (values.ndim - 1 - position))

    near = jax.random.permutation(own_key, shards_of)[block_of(target)]
    other_side = (block_of(target) + shards_of // 2) % shards_of
    return jnp.where((block_of(source) == near) | (block_of(source) == other_side), factor * values, values)


def block_scale(own_key, dims, cuts, least, top_value):
    gain, own = 1.0, jax.random.fold_in(own_key, 6)
    for position, blocks in cuts:
        heights = jnp.exp(jax.random.uniform(jax.random.fold_in(own, position), (blocks,), jnp.float32, least / len(cuts), top_value / len(cuts)))
        gain = gain * jnp.repeat(heights, dims[position] // blocks).reshape([-1 if axis == position else 1 for axis in range(len(dims))])
    return gain


def bell_draw(rng, extent, width, most, cuts=(), held_as=jnp.bfloat16):
    factor_of = block_scale(rng, extent, cuts, -0.22, 0.18) if cuts else 1.0
    drawn = jax.random.normal(rng, extent, jnp.float32) * width * factor_of
    return jnp.minimum(jnp.maximum(drawn, -most), most).astype(held_as)


def noise_with(own_key, dims, scale, bound, shards, heavy, kind=jnp.bfloat16):
    values = scale * jax.random.normal(own_key, dims, jnp.float32)
    if shards:
        values = values * block_scale(own_key, dims, shards, -0.22, 0.18)
    return jnp.clip(with_spikes(values, jax.random.fold_in(own_key, 3), *heavy), -bound, bound).astype(kind)


def setup_inputs(seed: int = 0) -> dict:
    streams_of = jax.random.split(jax.random.key(seed), 20)
    residual = draw_residual(jax.random.fold_in(streams_of[19], 71), 0)
    queries = draw_queries(jax.random.fold_in(streams_of[19], 71), 0)
    draft_token_keys = draw_draft_token_keys(jax.random.fold_in(streams_of[19], 71), 0)
    draft_token_values = bell_draw(streams_of[3], (ALL_TOKENS, KEY_VALUE_HEADS * HEAD_SIZE), 2.0, 8.0, ((1, 2),))
    cache_keys = draw_cache_keys(jax.random.fold_in(streams_of[19], 71), 0)
    cached_value_rows = bell_draw(streams_of[5], (TENANT_COUNT, CACHE_SLOTS, KEY_VALUE_HEADS * HEAD_SIZE), 2.0, 8.0, ((1, 16), (2, 2)))
    tenant_ids = draw_tenant_ids(jax.random.fold_in(streams_of[19], 71), 0)
    tree_mask = draw_tree_mask(jax.random.fold_in(streams_of[19], 71), 0)
    cache_lengths = jax.random.randint(streams_of[8], (TENANT_COUNT,), CACHE_SLOTS // 2 + 1, CACHE_SLOTS + 1).astype(jnp.int32)
    out_weight = bell_draw(streams_of[9], (QUERY_HEADS * HEAD_SIZE, D), (QUERY_HEADS * HEAD_SIZE) ** -0.5, 0.0625, ((0, 2), (1, 16)))
    out_signs = draw_out_signs(jax.random.fold_in(streams_of[19], 71), 0)
    norm_gain = jnp.clip(1.0 + 0.18 * jax.random.normal(streams_of[11], (D,), jnp.float32), 0.1, 1.9)
    gate_weight = bell_draw(streams_of[12], (D, FF), D ** -0.5, 0.0625, ((1, 32),))
    up_weight = bell_draw(streams_of[13], (D, FF), D ** -0.5, 0.0625, ((1, 32),))
    down_weight = noise_with(streams_of[14], (FF, D), FF ** -0.5, 0.09375, ((0, 32),), (0, 1, 32, 2.75))
    gate_signs = draw_gate_signs(jax.random.fold_in(streams_of[19], 71), 0)
    up_signs = draw_up_signs(jax.random.fold_in(streams_of[19], 71), 0)
    down_signs = draw_down_signs(jax.random.fold_in(streams_of[19], 71), 0)
    delta_scale = jnp.clip(jnp.exp(jax.random.uniform(streams_of[18], (TENANT_COUNT, 4), jnp.float32, math.log(0.3), math.log(0.9))), 0.3, 0.9)
    return dict(residual=residual, queries=queries, draft_token_keys=draft_token_keys, draft_token_values=draft_token_values, cache_keys=cache_keys, cached_value_rows=cached_value_rows, tenant_ids=tenant_ids, tree_mask=tree_mask, cache_lengths=cache_lengths, out_weight=out_weight, out_signs=out_signs, norm_gain=norm_gain, gate_weight=gate_weight, up_weight=up_weight, down_weight=down_weight, gate_signs=gate_signs, up_signs=up_signs, down_signs=down_signs, delta_scale=delta_scale)


NEG = -1e+30
EPS = 1e-05

def tenant_products(inputs, signs, factor):
    results = []
    for tenant_index in range(TENANT_COUNT):
        block_rows = inputs[tenant_index * DRAFT_TOKENS:(tenant_index + 1) * DRAFT_TOKENS]
        product = jnp.dot(block_rows, signs[tenant_index], preferred_element_type=jnp.float32)
        results.append(product * factor[tenant_index])
    return jnp.concatenate(results, axis=0)

def reference(residual, queries, draft_token_keys, draft_token_values, cache_keys, cached_value_rows, tenant_ids, tree_mask, cache_lengths, out_weight, out_signs, norm_gain, gate_weight, up_weight, down_weight, gate_signs, up_signs, down_signs, delta_scale):
    sort_order = jnp.argsort(tenant_ids, stable=True).astype(jnp.int32)
    inverse = jnp.argsort(sort_order).astype(jnp.int32)
    group_width = QUERY_HEADS // KEY_VALUE_HEADS
    factor = HEAD_SIZE ** (-0.5)
    ordered_queries = queries[sort_order].astype(jnp.float32).reshape(TENANT_COUNT, DRAFT_TOKENS, KEY_VALUE_HEADS, group_width, HEAD_SIZE)
    draft_key_lines = draft_token_keys[sort_order].astype(jnp.float32).reshape(ALL_TOKENS, KEY_VALUE_HEADS, HEAD_SIZE)
    draft_value_lines = draft_token_values[sort_order].astype(jnp.float32).reshape(ALL_TOKENS, KEY_VALUE_HEADS, HEAD_SIZE)
    visible = (tree_mask[sort_order][:, sort_order] > 0).reshape(TENANT_COUNT, DRAFT_TOKENS, 1, ALL_TOKENS)
    live = (jnp.arange(CACHE_SLOTS, dtype=jnp.int32)[None, :] < cache_lengths[:, None])[:, None, None, :]

    def single_group(index):
        query_part = lax.dynamic_index_in_dim(ordered_queries, index, 2, keepdims=False)
        keys_cache = lax.dynamic_slice_in_dim(cache_keys, index * HEAD_SIZE, HEAD_SIZE, 2).astype(jnp.float32)
        values_cache = lax.dynamic_slice_in_dim(cached_value_rows, index * HEAD_SIZE, HEAD_SIZE, 2).astype(jnp.float32)
        keys_draft = lax.dynamic_index_in_dim(draft_key_lines, index, 1, keepdims=False)
        values_draft = lax.dynamic_index_in_dim(draft_value_lines, index, 1, keepdims=False)
        cache_scores = jnp.einsum('tqwd,tjd->tqwj', query_part, keys_cache) * factor
        draft_scores = jnp.einsum('tqwd,kd->tqwk', query_part, keys_draft) * factor
        cache_masked = jnp.where(live, cache_scores, NEG)
        draft_masked = jnp.where(visible, draft_scores, NEG)
        peak = jnp.maximum(lax.optimization_barrier(jnp.max(cache_masked, axis=-1)), lax.optimization_barrier(jnp.max(draft_masked, axis=-1)))
        cache_weights = jnp.where(live, jnp.exp(cache_masked - peak[..., None]), 0.0)
        draft_weights = jnp.where(visible, jnp.exp(draft_masked - peak[..., None]), 0.0)
        total = lax.optimization_barrier(jnp.sum(cache_weights, axis=-1)) + lax.optimization_barrier(jnp.sum(draft_weights, axis=-1))
        cache_rounded = lax.optimization_barrier(cache_weights.astype(jnp.bfloat16)).astype(jnp.float32)
        draft_rounded = lax.optimization_barrier(draft_weights.astype(jnp.bfloat16)).astype(jnp.float32)
        combined = jnp.einsum('tqwj,tjd->tqwd', cache_rounded, values_cache)
        combined = combined + jnp.einsum('tqwk,kd->tqwd', draft_rounded, values_draft)
        return (combined / total[..., None]).astype(jnp.bfloat16)
    group_share = lax.map(single_group, jnp.arange(KEY_VALUE_HEADS, dtype=jnp.int32))
    attention = jnp.transpose(group_share, (1, 2, 0, 3, 4)).reshape(ALL_TOKENS, QUERY_HEADS * HEAD_SIZE)
    scales = delta_scale.astype(jnp.float32)
    projected = jnp.dot(attention, out_weight, preferred_element_type=jnp.float32)
    projected = projected + tenant_products(attention, out_signs, scales[:, 0] * (QUERY_HEADS * HEAD_SIZE) ** (-0.5))
    hidden = residual[sort_order].astype(jnp.float32) + projected
    normed = (hidden * lax.rsqrt(lax.optimization_barrier(jnp.mean(hidden * hidden, axis=1)) + EPS)[:, None] * norm_gain).astype(jnp.bfloat16)
    gate = jnp.dot(normed, gate_weight, preferred_element_type=jnp.float32)
    gate = gate + tenant_products(normed, gate_signs, scales[:, 1] * D ** (-0.5))
    up_part = jnp.dot(normed, up_weight, preferred_element_type=jnp.float32)
    up_part = up_part + tenant_products(normed, up_signs, scales[:, 2] * D ** (-0.5))
    active = (jax.nn.silu(gate) * up_part).astype(jnp.bfloat16)
    lowered = jnp.dot(active, down_weight, preferred_element_type=jnp.float32)
    lowered = lowered + tenant_products(active, down_signs, scales[:, 3] * FF ** (-0.5))
    return (hidden + lowered).astype(jnp.bfloat16)[inverse]
```

```python
import functools

import jax
import jax.numpy as jnp
from jax import lax
from jax.experimental import pallas as pl
from jax.experimental.pallas import tpu as pltpu
from jax.sharding import PartitionSpec as P

HEAD_SIZE = 128
LANES = 128
STAT_ROWS = 16
NEG = -1e30
EPS = 1e-05
F32 = jnp.float32
BF16 = jnp.bfloat16


def iota(shape, dim):
    return lax.broadcasted_iota(jnp.int32, shape, dim)


def to_row(column):
    rows = column.shape[0]
    diagonal = iota((rows, LANES), 0) == iota((rows, LANES), 1)
    return jnp.sum(jnp.where(diagonal, column, 0.0), axis=0, keepdims=True)


def to_column(row, rows):
    diagonal = iota((rows, LANES), 0) == iota((rows, LANES), 1)
    return jnp.sum(jnp.where(diagonal, row, 0.0), axis=1, keepdims=True)


def pack_stat(column):
    row = to_row(column)
    high = row.astype(BF16).astype(F32)
    middle = (row - high).astype(BF16).astype(F32)
    low = row - high - middle
    place = iota((STAT_ROWS, LANES), 0)
    packed = jnp.where(place == 0, high, jnp.where(place == 1, middle, low))
    return jnp.where(place < 3, packed, 0.0).astype(BF16)


def unpack_stat(block):
    return jnp.sum(block.astype(F32), axis=0, keepdims=True)


def reversed_bits(value, bits):
    out = 0
    for i in range(bits):
        out = out | (((value >> i) & 1) << (bits - 1 - i))
    return out


def whole(shape):
    zeros = (0,) * len(shape)
    return pl.BlockSpec(shape, lambda *_: zeros)


def attention_kernel(
    bits, tenants, me_ref, len_ref, tcol_ref, trow_ref, tree_ref, q_ref, dk_ref, dv_ref, k_ref,
    v_ref, out_ref, pm_ref,
):
    step = pl.program_id(0)
    tokens = tree_ref.shape[0]
    draft = tokens // tenants
    groups = pl.num_programs(0) // tenants
    tenant = step // groups
    me = me_ref[0]
    width = q_ref.shape[1] // HEAD_SIZE
    slots = k_ref.shape[1]
    rows = out_ref.shape[1] - STAT_ROWS
    all_rows = width * draft
    per_step = all_rows // rows

    @pl.when(step == 0)
    def _():
        tc = tcol_ref[...]
        tr = trow_ref[...]
        a = iota((tokens, tokens), 0)
        b = iota((tokens, tokens), 1)
        before = (tc < tr) | ((tc == tr) & (a < b))
        place = jnp.sum(before.astype(jnp.int32), axis=0, keepdims=True)
        pm_ref[...] = (place == a).astype(F32).astype(BF16)

    choose = pm_ref[pl.ds(pl.multiple_of(tenant * draft, draft), draft), :]
    mine = jnp.dot(choose, q_ref[...], preferred_element_type=F32).astype(BF16)
    query = jnp.concatenate(
        [mine[:, w * HEAD_SIZE : (w + 1) * HEAD_SIZE] for w in range(width)], axis=0
    )
    seen = jnp.dot(choose, tree_ref[...].astype(F32).astype(BF16), preferred_element_type=F32)
    seen = jnp.where(me == 0, seen, 0.0)
    seen = jnp.concatenate([seen] * width, axis=0) > 0.5
    live = me * slots + iota((1, slots), 1) < len_ref[tenant]
    factor = HEAD_SIZE ** (-0.5)
    nt = (((1,), (1,)), ((), ()))
    far = lax.dot_general(query, k_ref[0], nt, preferred_element_type=F32) * factor
    near = lax.dot_general(query, dk_ref[...], nt, preferred_element_type=F32) * factor
    far = jnp.where(live, far, NEG)
    near = jnp.where(seen, near, NEG)
    peak = jnp.maximum(
        jnp.max(far, axis=1, keepdims=True), jnp.max(near, axis=1, keepdims=True)
    )
    far = jnp.where(live, jnp.exp(far - peak), 0.0)
    near = jnp.where(seen, jnp.exp(near - peak), 0.0)
    total = jnp.sum(far, axis=1, keepdims=True) + jnp.sum(near, axis=1, keepdims=True)
    value = jnp.dot(far.astype(BF16), v_ref[0], preferred_element_type=F32) + jnp.dot(
        near.astype(BF16), dv_ref[...], preferred_element_type=F32
    )
    some = total > 0.0
    safe = jnp.where(some, total, 1.0)
    value = value / safe
    level = jnp.where(some, peak + jnp.log(safe), NEG)
    for part in range(per_step):
        block = step * per_step + part
        where = reversed_bits(block ^ me, bits)
        out_ref[where, :rows, :] = value[part * rows : (part + 1) * rows].astype(BF16)
        out_ref[where, rows:, :] = pack_stat(level[part * rows : (part + 1) * rows])


def attention_partials(me, lengths, tenant_ids, tree, queries, dk, dv, keys, values, n):
    tenants, slots, _ = keys.shape
    tokens = tenant_ids.shape[0]
    groups = dk.shape[1] // HEAD_SIZE
    width = queries.shape[1] // dk.shape[1]
    rows = tokens * groups * width // n
    bits = n.bit_length() - 1
    return pl.pallas_call(
        functools.partial(attention_kernel, bits, tenants),
        grid_spec=pltpu.PrefetchScalarGridSpec(
            num_scalar_prefetch=2,
            grid=(tenants * groups,),
            in_specs=[
                whole((tokens, 1)),
                whole((1, tokens)),
                whole((tokens, tokens)),
                pl.BlockSpec((tokens, width * HEAD_SIZE), lambda p, *_: (0, p % groups)),
                pl.BlockSpec((tokens, HEAD_SIZE), lambda p, *_: (0, p % groups)),
                pl.BlockSpec((tokens, HEAD_SIZE), lambda p, *_: (0, p % groups)),
                pl.BlockSpec((1, slots, HEAD_SIZE), lambda p, *_: (p // groups, 0, p % groups)),
                pl.BlockSpec((1, slots, HEAD_SIZE), lambda p, *_: (p // groups, 0, p % groups)),
            ],
            out_specs=[
                whole((n, rows + STAT_ROWS, HEAD_SIZE)),
                whole((tokens, tokens)),
            ],
        ),
        out_shape=[
            jax.ShapeDtypeStruct((n, rows + STAT_ROWS, HEAD_SIZE), BF16),
            jax.ShapeDtypeStruct((tokens, tokens), BF16),
        ],
        name="attention_partials",
    )(
        me, lengths, tenant_ids.reshape(tokens, 1), tenant_ids.reshape(1, tokens), tree, queries,
        dk, dv, keys, values,
    )


def merge_kernel(last, keep_ref, got_ref, *outs):
    count = got_ref.shape[0]
    rows = keep_ref.shape[1] - STAT_ROWS
    for i in range(count):
        a = unpack_stat(keep_ref[i, rows:, :])
        b = unpack_stat(got_ref[i, rows:, :])
        peak = jnp.maximum(a, b)
        ea = jnp.exp(a - peak)
        eb = jnp.exp(b - peak)
        total = ea + eb
        wa = to_column(ea / total, rows)
        value = keep_ref[i, :rows, :].astype(F32) * wa + got_ref[i, :rows, :].astype(F32) * (
            1.0 - wa
        )
        value = value.astype(BF16)
        if last:
            outs[0][i] = value
            continue
        level = peak + jnp.log(total)
        high = level.astype(BF16).astype(F32)
        middle = (level - high).astype(BF16).astype(F32)
        low = level - high - middle
        place = iota((STAT_ROWS, LANES), 0)
        packed = jnp.where(place == 0, high, jnp.where(place == 1, middle, low))
        packed = jnp.where(place < 3, packed, 0.0).astype(BF16)
        out, j = (outs[0], i) if i < count // 2 else (outs[1], i - count // 2)
        out[j, :rows, :] = value
        out[j, rows:, :] = packed


def merge(keep, got):
    count, tall, lanes = got.shape
    last = count == 1
    if last:
        shapes = [jax.ShapeDtypeStruct((1, tall - STAT_ROWS, lanes), BF16)]
    else:
        shapes = [jax.ShapeDtypeStruct((count // 2, tall, lanes), BF16)] * 2
    return pl.pallas_call(
        functools.partial(merge_kernel, last),
        in_specs=[pl.BlockSpec((count, tall, lanes), lambda: (0, 0, 0))] * 2,
        out_specs=[pl.BlockSpec(s.shape, lambda: (0, 0, 0)) for s in shapes],
        grid=(),
        out_shape=shapes,
        name="merge",
    )(keep, got)


def tenant_dot(x, w, s, scales):
    half = x.shape[0] // len(scales)
    delta = [
        jnp.dot(x[t * half : (t + 1) * half], s[t], preferred_element_type=F32) * scales[t]
        for t in range(len(scales))
    ]
    return jnp.dot(x, w, preferred_element_type=F32) + jnp.concatenate(delta, axis=0)


def out_kernel(bits, me_ref, scale_ref, rows_ref, w_ref, s_ref, o_ref, x_ref, acc_ref):
    step = pl.program_id(0)
    tenants = s_ref.shape[0]
    n, rows, _ = rows_ref.shape
    draft = x_ref.shape[1] // tenants
    deep = x_ref.shape[2]

    @pl.when(step == 0)
    def _():
        me = me_ref[0]
        heads = rows // draft
        for block in range(n):
            where = reversed_bits(block ^ me, bits)
            t, inside = divmod(block, n // tenants)
            for h in range(heads):
                chunk, column = divmod((inside * heads + h) * HEAD_SIZE, deep)
                x_ref[
                    chunk, t * draft : (t + 1) * draft, column : column + HEAD_SIZE
                ] = rows_ref[where, h * draft : (h + 1) * draft, :]
        acc_ref[...] = jnp.zeros_like(acc_ref)

    scales = [scale_ref[t] for t in range(tenants)]
    acc_ref[...] += tenant_dot(
        x_ref[step], w_ref[...], [s_ref[t] for t in range(tenants)], scales
    )

    @pl.when(step == pl.num_programs(0) - 1)
    def _():
        o_ref[...] = acc_ref[...].astype(BF16)


def out_projection(me, scale, rows, weight, signs, tokens):
    tenants = signs.shape[0]
    n = rows.shape[0]
    depth, features = weight.shape
    deep = min(512, depth)
    chunks = depth // deep
    return pl.pallas_call(
        functools.partial(out_kernel, n.bit_length() - 1),
        grid_spec=pltpu.PrefetchScalarGridSpec(
            num_scalar_prefetch=2,
            grid=(chunks,),
            in_specs=[
                whole(rows.shape),
                pl.BlockSpec((deep, features), lambda k, *_: (k, 0)),
                pl.BlockSpec((tenants, deep, features), lambda k, *_: (0, k, 0)),
            ],
            out_specs=whole((tokens, features)),
            scratch_shapes=[
                pltpu.VMEM((chunks, tokens, deep), BF16),
                pltpu.VMEM((tokens, features), F32),
            ],
        ),
        out_shape=jax.ShapeDtypeStruct((tokens, features), BF16),
        name="out_projection",
    )(me, scale, rows, weight, signs)


def hidden_kernel(pm_ref, residual_ref, own_ref, got_ref, gain_ref, hidden_ref, send_ref):
    tokens = own_ref.shape[0]
    hidden = jnp.dot(pm_ref[...], residual_ref[...], preferred_element_type=F32) + (
        own_ref[...].astype(F32) + got_ref[...].astype(F32)
    )
    hidden_ref[...] = hidden
    scaled = (hidden * gain_ref[...]).astype(BF16)
    pieces = hidden.shape[1] // LANES
    for f in range(pieces):
        send_ref[0, f * tokens : (f + 1) * tokens, :] = scaled[:, f * LANES : (f + 1) * LANES]
    send_ref[0, pieces * tokens :, :] = pack_stat(
        jnp.sum(hidden * hidden, axis=1, keepdims=True)
    )


def hidden_block(pm, residual, own, got, gain):
    tokens, features = own.shape
    tall = features // LANES * tokens + STAT_ROWS
    shapes = [
        jax.ShapeDtypeStruct((tokens, features), F32),
        jax.ShapeDtypeStruct((1, tall, LANES), BF16),
    ]
    return pl.pallas_call(
        hidden_kernel, out_shape=shapes, name="hidden_block"
    )(pm, residual, own, got, gain.reshape(1, features))


def gate_up_kernel(last, width, order_ref, scale_ref, x_ref, g_ref, u_ref, gs_ref, us_ref, *rest):
    step = pl.program_id(0)
    tenants = gs_ref.shape[0]
    if last:
        before_g, before_u, before_q, o_ref, acc_g, acc_u, acc_q = rest
    else:
        acc_g, acc_u, acc_q = rest

    @pl.when(step == 0)
    def _():
        if last:
            acc_g[...] = before_g[...]
            acc_u[...] = before_u[...]
            acc_q[...] = before_q[...]
        else:
            acc_g[...] = jnp.zeros_like(acc_g)
            acc_u[...] = jnp.zeros_like(acc_u)
            acc_q[...] = jnp.zeros_like(acc_q)

    tokens = acc_g.shape[0]
    pieces = (x_ref.shape[1] - STAT_ROWS) // tokens
    x = jnp.concatenate(
        [x_ref[0, f * tokens : (f + 1) * tokens, :] for f in range(pieces)], axis=1
    )
    acc_q[...] += x_ref[0, pieces * tokens :, :].astype(F32)
    for w, s, acc, row in ((g_ref, gs_ref, acc_g, 0), (u_ref, us_ref, acc_u, tenants)):
        scales = [scale_ref[row + t] for t in range(tenants)]
        acc[...] += tenant_dot(x, w[...], [s[t] for t in range(tenants)], scales)

    if last:

        @pl.when(step == pl.num_programs(0) - 1)
        def _():
            squares = jnp.sum(acc_q[...], axis=0, keepdims=True)
            norm = to_column(lax.rsqrt(squares / width + EPS), tokens)
            gate = acc_g[...] * norm
            up = acc_u[...] * norm
            o_ref[...] = (gate / (1.0 + jnp.exp(-gate)) * up).astype(BF16)


def gate_up(order, scale, x, gate, up, gate_signs, up_signs, tokens, before):
    count, tall, _ = x.shape
    tenants, depth, units = gate_signs.shape
    deep = (tall - STAT_ROWS) // tokens * LANES
    last = before is not None
    sums = [
        jax.ShapeDtypeStruct((tokens, units), F32),
        jax.ShapeDtypeStruct((tokens, units), F32),
        jax.ShapeDtypeStruct((STAT_ROWS, LANES), F32),
    ]
    weight_spec = pl.BlockSpec((deep, units), lambda i, order, *_: (order[i], 0))
    signs_spec = pl.BlockSpec((tenants, deep, units), lambda i, order, *_: (0, order[i], 0))
    in_specs = [
        pl.BlockSpec((1, tall, LANES), lambda i, *_: (i, 0, 0)),
        weight_spec,
        weight_spec,
        signs_spec,
        signs_spec,
    ]
    if last:
        in_specs += [whole(s.shape) for s in sums]
        shapes = jax.ShapeDtypeStruct((tokens, units), BF16)
        out_specs = whole((tokens, units))
        scratch = [pltpu.VMEM(s.shape, s.dtype) for s in sums]
    else:
        shapes, out_specs, scratch = sums, [whole(s.shape) for s in sums], []
    return pl.pallas_call(
        functools.partial(gate_up_kernel, last, depth),
        grid_spec=pltpu.PrefetchScalarGridSpec(
            num_scalar_prefetch=2,
            grid=(count,),
            in_specs=in_specs,
            out_specs=out_specs,
            scratch_shapes=scratch,
        ),
        out_shape=shapes,
        name="gate_up_last" if last else "gate_up_first",
    )(order, scale, x, gate, up, gate_signs, up_signs, *(before or ()))


def down_kernel(order_ref, scale_ref, x_ref, w_ref, s_ref, o_ref):
    tenants = s_ref.shape[0]
    scales = [scale_ref[t] for t in range(tenants)]
    o_ref[0] = tenant_dot(
        x_ref[...], w_ref[...], [s_ref[t] for t in range(tenants)], scales
    ).astype(BF16)


def down(order, scale, active, weight, signs, features):
    count = order.shape[0]
    tenants, units, _ = signs.shape
    tokens = active.shape[0]
    return pl.pallas_call(
        down_kernel,
        grid_spec=pltpu.PrefetchScalarGridSpec(
            num_scalar_prefetch=2,
            grid=(count,),
            in_specs=[
                whole(active.shape),
                pl.BlockSpec((units, features), lambda i, order, *_: (0, order[i])),
                pl.BlockSpec((tenants, units, features), lambda i, order, *_: (0, 0, order[i])),
            ],
            out_specs=pl.BlockSpec((1, tokens, features), lambda i, *_: (i, 0, 0)),
        ),
        out_shape=jax.ShapeDtypeStruct((count, tokens, features), BF16),
        name="down",
    )(order, scale, active, weight, signs)


def add_kernel(keep_ref, got_ref, *outs):
    count = got_ref.shape[0]
    total = (keep_ref[...].astype(F32) + got_ref[...].astype(F32)).astype(BF16)
    if len(outs) == 1:
        outs[0][...] = total
    else:
        outs[0][...] = total[: count // 2]
        outs[1][...] = total[count // 2 :]


def add(keep, got):
    count, tokens, features = got.shape
    outs = 1 if count == 1 else 2
    shape = jax.ShapeDtypeStruct((count // outs, tokens, features), BF16)
    return pl.pallas_call(add_kernel, out_shape=[shape] * outs, name="add")(keep, got)


def finish_kernel(pm_ref, hidden_ref, own_ref, got_ref, o_ref):
    mixed = hidden_ref[...] + (own_ref[0].astype(F32) + got_ref[0].astype(F32))
    o_ref[...] = lax.dot_general(
        pm_ref[...], mixed.astype(BF16), (((0,), (0,)), ((), ())), preferred_element_type=F32
    ).astype(BF16)


def finish(pm, hidden, own, got):
    return pl.pallas_call(
        finish_kernel, out_shape=jax.ShapeDtypeStruct(hidden.shape, BF16), name="finish"
    )(pm, hidden, own, got)


def shards(
    residual,
    queries,
    draft_token_keys,
    draft_token_values,
    cache_keys,
    cached_value_rows,
    tenant_ids,
    tree_mask,
    cache_lengths,
    out_weight,
    out_signs,
    norm_gain,
    gate_weight,
    up_weight,
    down_weight,
    gate_signs,
    up_signs,
    down_signs,
    delta_scale,
):
    n = lax.axis_size("ctx")
    bits = n.bit_length() - 1
    here = lax.axis_index("ctx").astype(jnp.int32)
    me = here.reshape(1)
    tokens = tenant_ids.shape[0]
    features = residual.shape[1]
    all_features = gate_weight.shape[0]
    all_units = gate_weight.shape[1] * n * lax.axis_size("kv")
    positions = jnp.array([reversed_bits(i, bits) for i in range(n)], jnp.int32)
    order = positions ^ here

    def swap(x, bit):
        return lax.ppermute(x, "ctx", [(i, i ^ (1 << bit)) for i in range(n)])

    def swap_kv(x):
        return lax.ppermute(x, "kv", [(0, 1), (1, 0)])

    partials, pm = attention_partials(
        me, cache_lengths, tenant_ids, tree_mask, queries, draft_token_keys, draft_token_values,
        cache_keys, cached_value_rows, n,
    )
    keep, send = partials[: n // 2], partials[n // 2 :]
    for bit in range(bits):
        got = swap(send, bit)
        merged = merge(keep, got)
        if bit < bits - 1:
            keep, send = merged
    rows = merged[0]
    for bit in reversed(range(bits)):
        rows = jnp.concatenate([rows, swap(rows, bit)], axis=0)

    own = out_projection(
        me, delta_scale[:, 0] * (out_weight.shape[0] * 2) ** (-0.5), rows, out_weight, out_signs,
        tokens,
    )
    hidden, block = hidden_block(pm, residual, own, swap_kv(own), norm_gain)

    for bit in reversed(range(1, bits)):
        block = jnp.concatenate([block, swap(block, bit)], axis=0)
    other = swap(block, 0)
    scale = delta_scale[:, 1:3].T.reshape(-1) * all_features ** (-0.5)
    sums = gate_up(
        order[: n // 2], scale, block, gate_weight, up_weight, gate_signs, up_signs, tokens, None
    )
    active = gate_up(
        order[n // 2 :], scale, other, gate_weight, up_weight, gate_signs, up_signs, tokens, sums
    )

    scale = delta_scale[:, 3] * all_units ** (-0.5)
    send = down(order[n // 2 :], scale, active, down_weight, down_signs, features)
    got = swap(send, 0)
    keep = down(order[: n // 2], scale, active, down_weight, down_signs, features)
    for bit in range(1, bits):
        keep, send = add(keep, got)
        got = swap(send, bit)
    (total,) = add(keep, got)
    return finish(pm, hidden, total, swap_kv(total))


def solution(mesh):
    return jax.shard_map(
        shards,
        mesh=mesh,
        in_specs=(
            P(None, "ctx"),
            P(None, "kv"),
            P(None, "kv"),
            P(None, "kv"),
            P(None, "ctx", "kv"),
            P(None, "ctx", "kv"),
            P(),
            P(),
            P(),
            P("kv", "ctx"),
            P(None, "kv", "ctx"),
            P("ctx"),
            P(None, ("kv", "ctx")),
            P(None, ("kv", "ctx")),
            P(("kv", "ctx"), None),
            P(None, None, ("kv", "ctx")),
            P(None, None, ("kv", "ctx")),
            P(None, ("kv", "ctx"), None),
            P(),
        ),
        out_specs=P(None, "ctx"),
        check_vma=False,
    )
```

```python
import functools

import jax
import jax.numpy as jnp
from jax import lax
from jax.experimental import pallas as pl
from jax.experimental.pallas import tpu as pltpu
from jax.sharding import PartitionSpec as P

HEAD_SIZE = 128
LANES = 128
STAT_ROWS = 16
NEG = -1e30
EPS = 1e-05
SLOTS = 4
MIB = 1 << 20
F32 = jnp.float32
BF16 = jnp.bfloat16


IN_VMEM = pl.BlockSpec(memory_space=pltpu.VMEM)
IN_SMEM = pl.BlockSpec(memory_space=pltpu.SMEM)
IN_HBM = pl.BlockSpec(memory_space=pl.ANY)


def vmem(x):
    return pltpu.with_memory_space_constraint(x, pltpu.VMEM)


def hbm(x):
    return pltpu.with_memory_space_constraint(x, pltpu.HBM)


def call(kernel, name, scalars, arrays, shapes, far=(), scratch=(), limit=4 * MIB, far_out=False):
    if far_out:
        out_shape = [jax.ShapeDtypeStruct(s, d) for s, d in shapes]
    else:
        out_shape = [pltpu.VMEM(s, d) for s, d in shapes]
    return pl.pallas_call(
        kernel,
        in_specs=[IN_SMEM] * len(scalars) + [IN_VMEM] * len(arrays) + [IN_HBM] * len(far),
        out_specs=[IN_VMEM] * len(shapes),
        out_shape=out_shape,
        scratch_shapes=list(scratch),
        compiler_params=pltpu.CompilerParams(vmem_limit_bytes=limit),
        name=name,
    )(*scalars, *[vmem(a) for a in arrays], *[hbm(a) for a in far])


def iota(shape, dim):
    return lax.broadcasted_iota(jnp.int32, shape, dim)


def to_row(column):
    rows = column.shape[0]
    diagonal = iota((rows, LANES), 0) == iota((rows, LANES), 1)
    return jnp.sum(jnp.where(diagonal, column, 0.0), axis=0, keepdims=True)


def to_column(row, rows):
    diagonal = iota((rows, LANES), 0) == iota((rows, LANES), 1)
    return jnp.sum(jnp.where(diagonal, row, 0.0), axis=1, keepdims=True)


def pack_row(row):
    high = row.astype(BF16).astype(F32)
    middle = (row - high).astype(BF16).astype(F32)
    low = row - high - middle
    place = iota((STAT_ROWS, LANES), 0)
    packed = jnp.where(place == 0, high, jnp.where(place == 1, middle, low))
    return jnp.where(place < 3, packed, 0.0).astype(BF16)


def unpack_row(block):
    return jnp.sum(block.astype(F32), axis=0, keepdims=True)


def reversed_bits(value, bits):
    out = 0
    for i in range(bits):
        out = out | (((value >> i) & 1) << (bits - 1 - i))
    return out


def attention_kernel(
    bits, me_ref, len_ref, ids_ref, tree_ref, q_ref, dk_ref, dv_ref, k_hbm, v_hbm, keep_ref,
    send_ref, pm_ref, k_ref, v_ref, sems,
):
    tenants, slots, _ = k_ref.shape
    copies = []
    for t in range(tenants):
        copies.append(
            (
                pltpu.make_async_copy(k_hbm.at[t], k_ref.at[t], sems.at[2 * t]),
                pltpu.make_async_copy(v_hbm.at[t], v_ref.at[t], sems.at[2 * t + 1]),
            )
        )
    for pair in copies:
        for copy in pair:
            copy.start()

    tokens = tree_ref.shape[0]
    draft = tokens // tenants
    groups = dk_ref.shape[1] // HEAD_SIZE
    width = q_ref.shape[1] // dk_ref.shape[1]
    me = me_ref[0]
    core = me & 1
    rows = keep_ref.shape[1] - STAT_ROWS
    parts = width * draft // rows
    factor = HEAD_SIZE ** (-0.5)
    nt = (((1,), (1,)), ((), ()))

    a = iota((tokens, tokens), 0)
    b = iota((tokens, tokens), 1)
    across = jnp.broadcast_to(ids_ref[...], (tokens, tokens))
    along = jnp.sum(jnp.where(a == b, across, 0), axis=1, keepdims=True)
    before = (along < across) | ((along == across) & (a < b))
    place = jnp.sum(before.astype(jnp.int32), axis=0, keepdims=True)
    choose = (place == a).astype(F32).astype(BF16)
    pm_ref[...] = choose
    seen_all = jnp.dot(choose, tree_ref[...].astype(F32).astype(BF16), preferred_element_type=F32)
    seen_all = jnp.where(me == 0, seen_all, 0.0)
    mine = jnp.dot(choose, q_ref[...], preferred_element_type=F32).astype(BF16)

    for t in range(tenants):
        seen = jnp.concatenate([seen_all[t * draft : (t + 1) * draft]] * width, axis=0) > 0.5
        live = me * slots + iota((1, slots), 1) < len_ref[t]
        for copy in copies[t]:
            copy.wait()
        for g in range(groups):
            head = slice(g * HEAD_SIZE, (g + 1) * HEAD_SIZE)
            query = jnp.concatenate(
                [
                    mine[
                        t * draft : (t + 1) * draft,
                        (g * width + w) * HEAD_SIZE : (g * width + w + 1) * HEAD_SIZE,
                    ]
                    for w in range(width)
                ],
                axis=0,
            )
            far = lax.dot_general(query, k_ref[t, :, head], nt, preferred_element_type=F32)
            near = lax.dot_general(query, dk_ref[:, head], nt, preferred_element_type=F32)
            far = jnp.where(live, far * factor, NEG)
            near = jnp.where(seen, near * factor, NEG)
            peak = jnp.maximum(
                jnp.max(far, axis=1, keepdims=True), jnp.max(near, axis=1, keepdims=True)
            )
            far = jnp.where(live, jnp.exp(far - peak), 0.0)
            near = jnp.where(seen, jnp.exp(near - peak), 0.0)
            total = jnp.sum(far, axis=1, keepdims=True) + jnp.sum(near, axis=1, keepdims=True)
            value = jnp.dot(far.astype(BF16), v_ref[t, :, head], preferred_element_type=F32)
            value = value + jnp.dot(near.astype(BF16), dv_ref[:, head], preferred_element_type=F32)
            some = total > 0.0
            safe = jnp.where(some, total, 1.0)
            value = value * (1.0 / safe)
            level = jnp.where(some, peak + jnp.log(safe), NEG)
            for i in range(0, parts, 2):
                even = value[i * rows : (i + 1) * rows]
                odd = value[(i + 1) * rows : (i + 2) * rows]
                even_level = to_row(level[i * rows : (i + 1) * rows])
                odd_level = to_row(level[(i + 1) * rows : (i + 2) * rows])
                block = (t * groups + g) * parts + i
                where = reversed_bits((block >> 1) ^ (me >> 1), bits - 1)
                first = core == 0
                keep_ref[where, :rows, :] = jnp.where(first, even, odd).astype(BF16)
                send_ref[where, :rows, :] = jnp.where(first, odd, even).astype(BF16)
                keep_ref[where, rows:, :] = pack_row(jnp.where(first, even_level, odd_level))
                send_ref[where, rows:, :] = pack_row(jnp.where(first, odd_level, even_level))


def attention_partials(me, lengths, tenant_ids, tree, queries, dk, dv, keys, values, n):
    tenants = keys.shape[0]
    tokens = tenant_ids.shape[0]
    groups = dk.shape[1] // HEAD_SIZE
    width = queries.shape[1] // dk.shape[1]
    rows = tokens * groups * width // n
    part = ((n // 2, rows + STAT_ROWS, HEAD_SIZE), BF16)
    return call(
        functools.partial(attention_kernel, n.bit_length() - 1),
        "attention_partials",
        [me, lengths],
        [tenant_ids.reshape(1, tokens), tree, queries, dk, dv],
        [part, part, ((tokens, tokens), BF16)],
        far=[keys, values],
        scratch=[
            pltpu.VMEM(keys.shape, BF16),
            pltpu.VMEM(values.shape, BF16),
            pltpu.SemaphoreType.DMA((2 * tenants,)),
        ],
        limit=12 * MIB,
    )


def merge_kernel(last, keep_ref, got_ref, token_ref, *outs):
    count = got_ref.shape[0]
    rows = keep_ref.shape[1] - STAT_ROWS
    for i in range(count):
        a = unpack_row(keep_ref[i, rows:, :])
        b = unpack_row(got_ref[i, rows:, :])
        peak = jnp.maximum(a, b)
        ea = jnp.exp(a - peak)
        eb = jnp.exp(b - peak)
        total = ea + eb
        wa = to_column(ea / total, rows)
        mine = keep_ref[i, :rows, :].astype(F32)
        value = got_ref[i, :rows, :].astype(F32)
        value = (value + (mine - value) * wa).astype(BF16)
        out, j = (outs[0], i) if last or i < count // 2 else (outs[1], i - count // 2)
        out[j, :rows, :] = value
        if not last:
            out[j, rows:, :] = pack_row(peak + jnp.log(total))


def merge(keep, got, token):
    count, tall, lanes = got.shape
    last = count == 1
    if last:
        shapes = [((1, tall - STAT_ROWS, lanes), BF16)]
    else:
        shapes = [((count // 2, tall, lanes), BF16)] * 2
    return call(
        functools.partial(merge_kernel, last), "merge", [], [keep, got, token], shapes
    )


def join_kernel(a_ref, b_ref, token_ref, o_ref):
    count = a_ref.shape[0]
    o_ref[:count] = a_ref[...]
    o_ref[count:] = b_ref[...]


def join(a, b, token):
    shape = (a.shape[0] + b.shape[0],) + a.shape[1:]
    return call(join_kernel, "join", [], [a, b, token], [(shape, a.dtype)])[0]


class Load:
    def __init__(self, source, scale, pieces, first, ordered, by_column, shape):
        self.source, self.scale, self.pieces, self.first = source, scale, pieces, first
        self.ordered, self.by_column, self.shape = ordered, by_column, shape

    def views(self, order_ref, w, s):
        rows, columns = self.shape
        for g in range(self.pieces):
            block = self.first + g
            if self.ordered:
                block = order_ref[block]
            if self.by_column:
                across = pl.ds(pl.multiple_of(block * columns, columns), columns)
                yield w.at[:, across], [s.at[t, :, across] for t in range(s.shape[0])]
            else:
                down = pl.ds(pl.multiple_of(block * rows, rows), rows)
                yield w.at[down], [s.at[t, down] for t in range(s.shape[0])]


def load_kernel(loads, n_sources, n_tokens, tenants, order_ref, scale_ref, *refs):
    tokens, refs = refs[:n_tokens], refs[n_tokens:]
    sources, refs = refs[: 2 * n_sources], refs[2 * n_sources :]
    outs, token_ref, refs = refs[: len(loads)], refs[len(loads)], refs[len(loads) + 1 :]
    token_ref[...] = jnp.zeros_like(token_ref)
    kinds = list(dict.fromkeys((l.pieces,) + l.shape for l in loads))
    buffers = {kind: (refs[2 * i], refs[2 * i + 1]) for i, kind in enumerate(kinds)}
    queue, seen = [], {kind: 0 for kind in kinds}
    for load, out in zip(loads, outs):
        kind = (load.pieces,) + load.shape
        buffer, sems = buffers[kind]
        slot = seen[kind] % SLOTS
        seen[kind] += 1
        copies = []
        w, s = sources[2 * load.source], sources[2 * load.source + 1]
        for g, (base, signs) in enumerate(load.views(order_ref, w, s)):
            for i, view in enumerate([base] + signs):
                copies.append(
                    pltpu.make_async_copy(
                        view, buffer.at[slot, i, g], sems.at[slot, g * (tenants + 1) + i]
                    )
                )
        queue.append((load, out, buffer, slot, copies))
    ahead = SLOTS
    for item in queue[:ahead]:
        for copy in item[-1]:
            copy.start()
    for i, (load, out, buffer, slot, copies) in enumerate(queue):
        for copy in copies:
            copy.wait()
        rows = load.shape[0]
        step = min(64, rows)
        scales = [scale_ref[load.scale * tenants + t] for t in range(tenants)]

        def combine(k, carry, out=out, buffer=buffer, slot=slot, scales=scales, load=load):
            at = pl.ds(pl.multiple_of(k * step, step), step)
            for g in range(load.pieces):
                base = buffer[slot, 0, g, at, :].astype(F32)
                for t in range(tenants):
                    sign = buffer[slot, 1 + t, g, at, :].astype(F32)
                    out[g, t, at, :] = (base + scales[t] * sign).astype(BF16)
            return carry

        lax.fori_loop(0, rows // step, combine, 0)
        if i + ahead < len(queue):
            for copy in queue[i + ahead][-1]:
                copy.start()


def load(order, scale, loads, sources, tokens, tenants):
    used = sorted({l.source for l in loads})
    loads = [
        Load(used.index(l.source), l.scale, l.pieces, l.first, l.ordered, l.by_column, l.shape)
        for l in loads
    ]
    far = [x for i in used for x in sources[i]]
    kinds = list(dict.fromkeys((l.pieces,) + l.shape for l in loads))
    scratch = []
    for pieces, rows, columns in kinds:
        scratch.append(pltpu.VMEM((SLOTS, tenants + 1, pieces, rows, columns), BF16))
        scratch.append(pltpu.SemaphoreType.DMA((SLOTS, pieces * (tenants + 1))))
    shapes = [((l.pieces, tenants) + l.shape, BF16) for l in loads] + [((8, LANES), F32)]
    *blocks, token = call(
        functools.partial(load_kernel, loads, len(used), len(tokens), tenants),
        "load",
        [order, scale],
        tokens,
        shapes,
        far=far,
        scratch=scratch,
        limit=(7 * len(kinds)) * MIB,
    )
    return blocks, token


def out_kernel(bits, me_ref, low_ref, high_ref, *rest):
    *w_refs, o_ref, all_ref, x_ref = rest
    half, rows, _ = low_ref.shape
    n = 2 * half
    tenants = w_refs[0].shape[1]
    draft = x_ref.shape[0] // tenants
    me = me_ref[0]
    all_ref[:half] = low_ref[...]
    all_ref[half:] = high_ref[...]
    heads = rows // draft
    for block in range(n):
        where = reversed_bits(block ^ me, bits)
        t, inside = divmod(block, n // tenants)
        for h in range(heads):
            column = (inside * heads + h) * HEAD_SIZE
            x_ref[t * draft : (t + 1) * draft, column : column + HEAD_SIZE] = all_ref[
                where, h * draft : (h + 1) * draft, :
            ]
    for t in range(tenants):
        total, at = 0.0, 0
        for w in w_refs:
            deep = w.shape[2]
            total = total + jnp.dot(
                x_ref[t * draft : (t + 1) * draft, at : at + deep],
                w[0, t],
                preferred_element_type=F32,
            )
            at += deep
        o_ref[t * draft : (t + 1) * draft, :] = total.astype(BF16)


def out_projection(me, low, high, weights, tokens):
    half, rows, lanes = low.shape
    features = weights[0].shape[-1]
    depth = sum(w.shape[2] for w in weights)
    return call(
        functools.partial(out_kernel, (2 * half).bit_length() - 1),
        "out_projection",
        [me],
        [low, high] + weights,
        [((tokens, features), BF16)],
        scratch=[pltpu.VMEM((2 * half, rows, lanes), BF16), pltpu.VMEM((tokens, depth), BF16)],
    )[0]


def hidden_kernel(pm_ref, residual_ref, gain_ref, own_ref, got_ref, token_ref, hidden_ref, send_ref):
    tokens = own_ref.shape[0]
    hidden = jnp.dot(pm_ref[...], residual_ref[...], preferred_element_type=F32) + (
        own_ref[...].astype(F32) + got_ref[...].astype(F32)
    )
    hidden_ref[...] = hidden
    scaled = (hidden * gain_ref[...]).astype(BF16)
    pieces = hidden.shape[1] // LANES
    for f in range(pieces):
        send_ref[0, f * tokens : (f + 1) * tokens, :] = scaled[:, f * LANES : (f + 1) * LANES]
    squares = jnp.sum(hidden * hidden, axis=1, keepdims=True)
    send_ref[0, pieces * tokens :, :] = pack_row(to_row(squares))


def hidden_block(pm, residual, gain, own, got, token):
    tokens, features = own.shape
    tall = features // LANES * tokens + STAT_ROWS
    return call(
        hidden_kernel,
        "hidden_block",
        [],
        [pm, residual, gain.reshape(1, features), own, got, token],
        [((tokens, features), F32), ((1, tall, LANES), BF16)],
    )


def gate_up_kernel(stage, n_weights, width, x_ref, token_ref, *rest):
    g_refs, u_refs, rest = rest[:n_weights], rest[n_weights : 2 * n_weights], rest[2 * n_weights :]
    if stage > 0:
        before, rest = rest[:3], rest[3:]
    tokens = rest[0].shape[0]
    tenants = g_refs[0].shape[1]
    draft = tokens // tenants
    count = x_ref.shape[0]
    columns = (x_ref.shape[1] - STAT_ROWS) // tokens
    squares = jnp.zeros((STAT_ROWS, LANES), F32)
    for i in range(count):
        squares = squares + x_ref[i, columns * tokens :, :].astype(F32)
    if stage > 0:
        squares = squares + before[2][...]
    if stage == 2:
        norm = to_column(
            lax.rsqrt(jnp.sum(squares, axis=0, keepdims=True) / width + EPS), tokens
        )
    else:
        rest[2][...] = squares
    for t in range(tenants):
        own = slice(t * draft, (t + 1) * draft)
        sums = [before[j][own, :] if stage > 0 else 0.0 for j in range(2)]
        for i in range(count):
            x = jnp.concatenate(
                [
                    x_ref[i, f * tokens + t * draft : f * tokens + (t + 1) * draft, :]
                    for f in range(columns)
                ],
                axis=1,
            )
            job, piece = divmod(i, g_refs[0].shape[0])
            for j, refs in enumerate((g_refs, u_refs)):
                sums[j] = sums[j] + jnp.dot(x, refs[job][piece, t], preferred_element_type=F32)
        if stage < 2:
            rest[0][own, :] = sums[0]
            rest[1][own, :] = sums[1]
        else:
            gate = sums[0] * norm[own]
            up = sums[1] * norm[own]
            rest[0][own, :] = (gate / (1.0 + jnp.exp(-gate)) * up).astype(BF16)


def gate_up(stage, x, token, gates, ups, tokens, width, before=()):
    units = gates[0].shape[-1]
    if stage < 2:
        shapes = [((tokens, units), F32)] * 2 + [((STAT_ROWS, LANES), F32)]
    else:
        shapes = [((tokens, units), BF16)]
    return call(
        functools.partial(gate_up_kernel, stage, len(gates), width),
        f"gate_up_{stage}",
        [],
        [x, token] + gates + ups + list(before),
        shapes,
    )


def down_kernel(x_ref, token_ref, *rest):
    *w_refs, o_ref = rest
    pieces, tenants = w_refs[0].shape[:2]
    draft = x_ref.shape[0] // tenants
    for i in range(o_ref.shape[0]):
        job, piece = divmod(i, pieces)
        for t in range(tenants):
            own = slice(t * draft, (t + 1) * draft)
            o_ref[i, own, :] = jnp.dot(
                x_ref[own, :], w_refs[job][piece, t], preferred_element_type=F32
            ).astype(BF16)


def down(active, token, weights):
    pieces, _, _, features = weights[0].shape
    tokens = active.shape[0]
    shape = (pieces * len(weights), tokens, features)
    return call(down_kernel, "down", [], [active, token] + weights, [(shape, BF16)])[0]


def add_kernel(keep_ref, got_ref, *outs):
    count = got_ref.shape[0]
    for i in range(count):
        total = (keep_ref[i].astype(F32) + got_ref[i].astype(F32)).astype(BF16)
        out, j = (outs[0], i) if count == 1 or i < count // 2 else (outs[1], i - count // 2)
        out[j] = total


def add(keep, got):
    count, tokens, features = got.shape
    outs = 1 if count == 1 else 2
    return call(
        add_kernel, "add", [], [keep, got], [((count // outs, tokens, features), BF16)] * outs
    )


def finish_kernel(pm_ref, hidden_ref, own_ref, got_ref, o_ref):
    mixed = hidden_ref[...] + (own_ref[0].astype(F32) + got_ref[0].astype(F32))
    o_ref[...] = lax.dot_general(
        pm_ref[...], mixed.astype(BF16), (((0,), (0,)), ((), ())), preferred_element_type=F32
    ).astype(BF16)


def finish(pm, hidden, own, got):
    return call(
        finish_kernel, "finish", [], [pm, hidden, own, got], [(hidden.shape, BF16)], far_out=True
    )[0]


def shards(
    residual,
    queries,
    draft_token_keys,
    draft_token_values,
    cache_keys,
    cached_value_rows,
    tenant_ids,
    tree_mask,
    cache_lengths,
    out_weight,
    out_signs,
    norm_gain,
    gate_weight,
    up_weight,
    down_weight,
    gate_signs,
    up_signs,
    down_signs,
    delta_scale,
):
    n = lax.axis_size("ctx")
    bits = n.bit_length() - 1
    here = lax.axis_index("ctx").astype(jnp.int32)
    me = here.reshape(1)
    tokens = tenant_ids.shape[0]
    tenants = cache_keys.shape[0]
    features = residual.shape[1]
    all_features, units = gate_weight.shape
    depth = out_weight.shape[0]
    n_kv = lax.axis_size("kv")
    order = jnp.array([reversed_bits(i, bits) for i in range(n)], jnp.int32) ^ here
    widths = jnp.array([depth * n_kv, all_features, all_features, units * n * n_kv], F32)
    scale = (delta_scale.T * widths[:, None] ** (-0.5)).reshape(-1)

    def swap(x, bit):
        return lax.ppermute(x, "ctx", [(i, i ^ (1 << bit)) for i in range(n)])

    def swap_kv(x):
        return lax.ppermute(x, "kv", [(i, (i + 1) % n_kv) for i in range(n_kv)])

    sources = [
        (out_weight, out_signs),
        (gate_weight, gate_signs),
        (up_weight, up_signs),
        (down_weight, down_signs),
    ]
    pieces = max(1, n // 16)
    deep = min(512, depth)
    todo = [
        (("out", i), Load(0, 0, 1, i, False, False, (deep, features)))
        for i in range(depth // deep)
    ]
    for i in range(0, n, pieces):
        todo.append((("gate", i), Load(1, 1, pieces, i, True, False, (features, units))))
        todo.append((("up", i), Load(2, 2, pieces, i, True, False, (features, units))))
    n_before = len(todo)
    for i in list(range(n // 2, n, pieces)) + list(range(0, n // 2, pieces)):
        todo.append((("down", i), Load(3, 3, pieces, i, True, True, (units, features))))
    held = {}

    def fill(count, *tokens_in):
        nonlocal todo
        now, todo = todo[:count], todo[count:]
        if not now:
            return jnp.zeros((8, LANES), F32)
        blocks, token = load(order, scale, [l for _, l in now], sources, list(tokens_in), tenants)
        for (name, _), block in zip(now, blocks):
            held[name] = block
        return token

    keep, send, pm = attention_partials(
        me, cache_lengths, tenant_ids, tree_mask, queries, draft_token_keys, draft_token_values,
        cache_keys, cached_value_rows, n,
    )
    plan = PLAN_DOWN[:bits] + [0] * (bits - len(PLAN_DOWN))
    for bit in range(bits):
        got = swap(send, bit)
        token = fill(plan[bit], send)
        merged = merge(keep, got, token)
        if bit < bits - 1:
            keep, send = merged
    rows = merged[0]
    plan = [0] * (bits - len(PLAN_UP)) + PLAN_UP[-bits:]
    for bit in reversed(range(1, bits)):
        got = swap(rows, bit)
        token = fill(plan[bits - 1 - bit], rows)
        rows = join(rows, got, token)
    other = swap(rows, 0)
    left = n_before - (len(held))
    token = fill(left, rows)

    names = [name for name in held if name[0] == "out"]
    own = out_projection(me, rows, other, [held[name] for name in names], tokens)
    got = swap_kv(own)
    token = fill(PLAN_LAST[0], own)
    hidden, block = hidden_block(pm, residual, norm_gain, own, got, token)

    def blocks_of(kind, first, end):
        return [held[kind, i] for i in range(first, end, pieces)]

    for bit in reversed(range(2, bits)):
        got = swap(block, bit)
        last = bit == 2
        token = fill(len(todo) if last else PLAN_LAST[1], block)
        block = join(block, got, token)
    quarter, half = n // 4, n // 2
    got = swap(block, 1)
    sums = gate_up(
        0, block, token, blocks_of("gate", 0, quarter), blocks_of("up", 0, quarter), tokens,
        all_features,
    )
    block = join(block, got, sums[2])
    other = swap(block, 0)
    sums = gate_up(
        1, got, sums[2], blocks_of("gate", quarter, half), blocks_of("up", quarter, half), tokens,
        all_features, sums,
    )
    (active,) = gate_up(
        2, other, sums[2], blocks_of("gate", half, n), blocks_of("up", half, n), tokens,
        all_features, sums,
    )

    send = down(active, token, blocks_of("down", half, n))
    got = swap(send, 0)
    keep = down(active, send, blocks_of("down", 0, half))
    for bit in range(1, bits):
        keep, send = add(keep, got)
        got = swap(send, bit)
    (total,) = add(keep, got)
    return finish(pm, hidden, total, swap_kv(total))


PLAN_DOWN = [2, 8, 5, 6]
PLAN_UP = [6, 5, 6]
PLAN_LAST = [4, 6]


def solution(mesh):
    return jax.shard_map(
        shards,
        mesh=mesh,
        in_specs=(
            P(None, "ctx"),
            P(None, "kv"),
            P(None, "kv"),
            P(None, "kv"),
            P(None, "ctx", "kv"),
            P(None, "ctx", "kv"),
            P(),
            P(),
            P(),
            P("kv", "ctx"),
            P(None, "kv", "ctx"),
            P("ctx"),
            P(None, ("kv", "ctx")),
            P(None, ("kv", "ctx")),
            P(("kv", "ctx"), None),
            P(None, None, ("kv", "ctx")),
            P(None, None, ("kv", "ctx")),
            P(None, ("kv", "ctx"), None),
            P(),
        ),
        out_specs=P(None, "ctx"),
        check_vma=False,
    )
```

```python
import functools

import jax
import jax.numpy as jnp
from jax import lax
from jax.experimental import pallas as pl
from jax.experimental.pallas import tpu as pltpu
from jax.sharding import PartitionSpec as P

HEAD_SIZE = 128
LANES = 128
STAT_ROWS = 16
NEG = -1e30
EPS = 1e-05
LOG2E = 1.4426950408889634
SLOTS = 4
MIB = 1 << 20
F32 = jnp.float32
BF16 = jnp.bfloat16


IN_VMEM = pl.BlockSpec(memory_space=pltpu.VMEM)
IN_SMEM = pl.BlockSpec(memory_space=pltpu.SMEM)
IN_HBM = pl.BlockSpec(memory_space=pl.ANY)


def vmem(x):
    return pltpu.with_memory_space_constraint(x, pltpu.VMEM)


def hbm(x):
    return pltpu.with_memory_space_constraint(x, pltpu.HBM)


def call(kernel, scalars, arrays, shapes, far=(), scratch=(), limit=4 * MIB, far_out=False):
    if far_out:
        out_shape = [jax.ShapeDtypeStruct(s, d) for s, d in shapes]
    else:
        out_shape = [pltpu.VMEM(s, d) for s, d in shapes]
    return pl.pallas_call(
        kernel,
        in_specs=[IN_SMEM] * len(scalars) + [IN_VMEM] * len(arrays) + [IN_HBM] * len(far),
        out_specs=[IN_VMEM] * len(shapes),
        out_shape=out_shape,
        scratch_shapes=list(scratch),
        compiler_params=pltpu.CompilerParams(vmem_limit_bytes=limit),
    )(*scalars, *[vmem(a) for a in arrays], *[hbm(a) for a in far])


def iota(shape, dim):
    return lax.broadcasted_iota(jnp.int32, shape, dim)


def to_row(column):
    rows = column.shape[0]
    diagonal = iota((rows, LANES), 0) == iota((rows, LANES), 1)
    return jnp.sum(jnp.where(diagonal, column, 0.0), axis=0, keepdims=True)


def to_column(row, rows):
    diagonal = iota((rows, LANES), 0) == iota((rows, LANES), 1)
    return jnp.sum(jnp.where(diagonal, row, 0.0), axis=1, keepdims=True)


def pack_row(row):
    high = row.astype(BF16).astype(F32)
    middle = (row - high).astype(BF16).astype(F32)
    low = row - high - middle
    place = iota((STAT_ROWS, LANES), 0)
    packed = jnp.where(place == 0, high, jnp.where(place == 1, middle, low))
    return jnp.where(place < 3, packed, 0.0).astype(BF16)


def unpack_row(block):
    return jnp.sum(block.astype(F32), axis=0, keepdims=True)


def reversed_bits(value, bits):
    out = 0
    for i in range(bits):
        out = out | (((value >> i) & 1) << (bits - 1 - i))
    return out


def start_halves(copies, rows):
    def half(h, carry):
        for copy in copies(pl.multiple_of(h * (rows // 2), rows // 2), rows // 2):
            copy.start()
        return carry

    lax.fori_loop(0, 2, half, 0)


def attention_kernel(bits, n_raw, me_ref, len_ref, *refs):
    ids_hbm, tree_hbm, q_hbm, dk_hbm, dv_hbm, k_hbm, v_hbm, res_hbm, gain_hbm, w_hbm, s_hbm = refs[:11]
    keep_ref, send_ref, pm_ref, res_ref, gain_ref = refs[11:16]
    raw_refs = refs[16 : 16 + n_raw]
    ids_ref, tree_ref, q_ref, dk_ref, dv_ref, k_ref, v_ref, sems, raw_sems = refs[16 + n_raw :]
    tenants, slots, _ = k_ref.shape
    small = [
        pltpu.make_async_copy(source, target, sems.at[i])
        for i, (source, target) in enumerate(
            [
                (ids_hbm, ids_ref), (tree_hbm, tree_ref), (q_hbm, q_ref), (dk_hbm, dk_ref),
                (dv_hbm, dv_ref), (res_hbm, res_ref), (gain_hbm, gain_ref),
            ]
        )
    ]
    cache = []
    for t in range(tenants):
        at = len(small) + 2 * t
        cache.append(
            [
                pltpu.make_async_copy(k_hbm.at[t], k_ref.at[t], sems.at[at]),
                pltpu.make_async_copy(v_hbm.at[t], v_ref.at[t], sems.at[at + 1]),
            ]
        )

    def raw_copies(first, rows):
        for i, out in enumerate(raw_refs):
            at, to = pl.ds(i * out.shape[2] + first, rows), pl.ds(first, rows)
            yield pltpu.make_async_copy(w_hbm.at[at], out.at[0, 0, to], raw_sems.at[i, 0])
            for t in range(tenants):
                yield pltpu.make_async_copy(
                    s_hbm.at[t, at], out.at[0, 1 + t, to], raw_sems.at[i, 1 + t]
                )

    for copy in small + [c for pair in cache for c in pair]:
        copy.start()

    tokens = tree_ref.shape[0]
    draft = tokens // tenants
    groups = dk_ref.shape[1] // HEAD_SIZE
    width = q_ref.shape[1] // dk_ref.shape[1]
    me = me_ref[0]
    core = me & 1
    rows = keep_ref.shape[1] - STAT_ROWS
    parts = width * draft // rows
    factor = HEAD_SIZE ** (-0.5)
    power = factor * LOG2E
    nt = (((1,), (1,)), ((), ()))

    for copy in small:
        copy.wait()
    a = iota((tokens, tokens), 0)
    b = iota((tokens, tokens), 1)
    across = jnp.broadcast_to(ids_ref[...], (tokens, tokens))
    along = jnp.sum(jnp.where(a == b, across, 0), axis=1, keepdims=True)
    before = (along < across) | ((along == across) & (a < b))
    place = jnp.sum(before.astype(jnp.int32), axis=0, keepdims=True)
    choose = (place == a).astype(F32).astype(BF16)
    pm_ref[...] = choose
    seen_all = jnp.dot(choose, tree_ref[...].astype(F32).astype(BF16), preferred_element_type=F32)
    seen_all = jnp.where(me == 0, seen_all, 0.0)
    mine = jnp.dot(choose, q_ref[...], preferred_element_type=F32).astype(BF16)

    for t in range(tenants):
        seen = jnp.concatenate([seen_all[t * draft : (t + 1) * draft]] * width, axis=0) > 0.5
        live = me * slots + iota((1, slots), 1) < len_ref[t]
        for copy in cache[t]:
            copy.wait()
        if t == 0:
            start_halves(raw_copies, raw_refs[0].shape[2])
        for g in range(groups):
            head = slice(g * HEAD_SIZE, (g + 1) * HEAD_SIZE)
            query = jnp.concatenate(
                [
                    mine[
                        t * draft : (t + 1) * draft,
                        (g * width + w) * HEAD_SIZE : (g * width + w + 1) * HEAD_SIZE,
                    ]
                    for w in range(width)
                ],
                axis=0,
            )
            far = lax.dot_general(query, k_ref[t, :, head], nt, preferred_element_type=F32)
            near = lax.dot_general(query, dk_ref[:, head], nt, preferred_element_type=F32)
            far = jnp.where(live, far, NEG)
            near = jnp.where(seen, near, NEG)
            peak = jnp.maximum(
                jnp.max(far, axis=1, keepdims=True), jnp.max(near, axis=1, keepdims=True)
            )
            some = peak > 0.5 * NEG
            far = jnp.exp2((far - peak) * power)
            near = jnp.exp2((near - peak) * power)
            total = jnp.sum(far, axis=1, keepdims=True) + jnp.sum(near, axis=1, keepdims=True)
            value = jnp.dot(far.astype(BF16), v_ref[t, :, head], preferred_element_type=F32)
            value = value + jnp.dot(near.astype(BF16), dv_ref[:, head], preferred_element_type=F32)
            value = value * (1.0 / total)
            level = jnp.where(some, peak * factor + jnp.log(total), NEG)
            for i in range(0, parts, 2):
                even = value[i * rows : (i + 1) * rows]
                odd = value[(i + 1) * rows : (i + 2) * rows]
                even_level = to_row(level[i * rows : (i + 1) * rows])
                odd_level = to_row(level[(i + 1) * rows : (i + 2) * rows])
                block = (t * groups + g) * parts + i
                where = reversed_bits((block >> 1) ^ (me >> 1), bits - 1)
                first = core == 0
                keep_ref[where, :rows, :] = jnp.where(first, even, odd).astype(BF16)
                send_ref[where, :rows, :] = jnp.where(first, odd, even).astype(BF16)
                keep_ref[where, rows:, :] = pack_row(jnp.where(first, even_level, odd_level))
                send_ref[where, rows:, :] = pack_row(jnp.where(first, odd_level, even_level))
    for copy in raw_copies(0, raw_refs[0].shape[2]):
        copy.wait()


def attention_partials(
    me, lengths, tenant_ids, tree, queries, dk, dv, keys, values, residual, gain, weight, signs, n
):
    tenants = keys.shape[0]
    tokens = tenant_ids.shape[0]
    groups = dk.shape[1] // HEAD_SIZE
    width = queries.shape[1] // dk.shape[1]
    rows = tokens * groups * width // n
    depth, features = weight.shape
    deep = min(512, depth)
    n_raw = depth // deep
    part = ((n // 2, rows + STAT_ROWS, HEAD_SIZE), BF16)
    gain = gain.reshape(1, features)
    ids = tenant_ids.reshape(1, tokens)
    inner = [ids, tree, queries, dk, dv, keys, values]
    return call(
        functools.partial(attention_kernel, n.bit_length() - 1, n_raw),
        [me, lengths],
        [],
        [part, part, ((tokens, tokens), BF16), (residual.shape, BF16), (gain.shape, F32)]
        + [((1, 1 + tenants, deep, features), BF16)] * n_raw,
        far=inner + [residual, gain, weight, signs],
        scratch=[pltpu.VMEM(x.shape, x.dtype) for x in inner]
        + [
            pltpu.SemaphoreType.DMA((7 + 2 * tenants,)),
            pltpu.SemaphoreType.DMA((n_raw, 1 + tenants)),
        ],
        limit=12 * MIB,
    )


def merged(a_ref, i, b_ref, j, rows):
    a = unpack_row(a_ref[i, rows:, :])
    b = unpack_row(b_ref[j, rows:, :])
    peak = jnp.maximum(a, b)
    ea = jnp.exp(a - peak)
    eb = jnp.exp(b - peak)
    total = ea + eb
    wa = to_column(ea / total, rows)
    mine = a_ref[i, :rows, :].astype(F32)
    value = b_ref[j, :rows, :].astype(F32)
    return (value + (mine - value) * wa).astype(BF16), peak + jnp.log(total)


def merge_kernel(keep_ref, got_ref, token_ref, *outs):
    count = got_ref.shape[0]
    rows = keep_ref.shape[1] - STAT_ROWS
    for i in range(count):
        value, level = merged(keep_ref, i, got_ref, i, rows)
        per_out = count // len(outs)
        out, j = outs[i // per_out], i % per_out
        out[j, :rows, :] = value
        out[j, rows:, :] = pack_row(level)


def merge(keep, got, token):
    count, tall, lanes = got.shape
    outs = 1 if count == 2 else 2
    shapes = [((count // outs, tall, lanes), BF16)] * outs
    return call(merge_kernel, [], [keep, got, token], shapes)


def finish_rows_kernel(own_ref, got_ref, token_ref, o_ref):
    rows = o_ref.shape[1]
    for i in range(2):
        o_ref[i] = merged(own_ref, i, got_ref, 1 - i, rows)[0]


def finish_rows(own, got, token):
    _, tall, lanes = own.shape
    return call(
        finish_rows_kernel, [], [own, got, token],
        [((2, tall - STAT_ROWS, lanes), BF16)],
    )[0]


def join_kernel(a_ref, b_ref, token_ref, o_ref):
    count = a_ref.shape[0]
    o_ref[:count] = a_ref[...]
    o_ref[count:] = b_ref[...]


def join(a, b, token):
    shape = (a.shape[0] + b.shape[0],) + a.shape[1:]
    return call(join_kernel, [], [a, b, token], [(shape, a.dtype)])[0]


class Load:
    def __init__(self, source, kind, scale, pieces, first, ordered, by_column, shape):
        self.source, self.kind, self.scale = source, kind, scale
        self.pieces, self.first = pieces, first
        self.ordered, self.by_column, self.shape = ordered, by_column, shape

    def views(self, me, bits, w, s, first=0, count=None):
        rows, columns = self.shape
        count = count or rows
        for g in range(self.pieces):
            block = self.first + g
            if self.ordered:
                block = reversed_bits(block, bits) ^ me
            if self.by_column:
                at = (
                    pl.ds(first, count),
                    pl.ds(pl.multiple_of(block * columns, columns), columns),
                )
            else:
                at = (pl.ds(pl.multiple_of(block * rows, rows) + first, count),)
            yield w.at[at], [s.at[(t,) + at] for t in range(s.shape[0])]


def load_kernel(bits, loads, n_sources, n_tokens, tenants, me_ref, scale_ref, *refs):
    me = me_ref[0]
    refs = refs[n_tokens:]
    sources, refs = refs[: 2 * n_sources], refs[2 * n_sources :]
    outs, token_ref, refs = refs[: len(loads)], refs[len(loads)], refs[len(loads) + 1 :]
    token_ref[...] = jnp.zeros_like(token_ref)
    kinds = list(dict.fromkeys((l.pieces,) + l.shape for l in loads))
    buffers = {kind: (refs[2 * i], refs[2 * i + 1]) for i, kind in enumerate(kinds)}
    queue, seen = [], {kind: 0 for kind in kinds}
    for load, out in zip(loads, outs):
        kind = (load.pieces,) + load.shape
        buffer, sems = buffers[kind]
        slot = seen[kind] % SLOTS
        seen[kind] += 1
        copies = []
        w, s = sources[2 * load.source], sources[2 * load.source + 1]
        for g, (base, signs) in enumerate(load.views(me, bits, w, s)):
            for i, view in enumerate([base] + signs):
                copies.append(
                    pltpu.make_async_copy(
                        view, buffer.at[slot, i, g], sems.at[slot, g * (tenants + 1) + i]
                    )
                )
        queue.append((load, out, buffer, slot, copies))
    ahead = SLOTS
    for item in queue[:ahead]:
        for copy in item[-1]:
            copy.start()
    for i, (load, out, buffer, slot, copies) in enumerate(queue):
        for copy in copies:
            copy.wait()
        rows = load.shape[0]
        step = min(64, rows)
        scales = [scale_ref[t, load.kind] * load.scale for t in range(tenants)]

        def combine(k, carry, out=out, buffer=buffer, slot=slot, scales=scales, load=load):
            at = pl.ds(pl.multiple_of(k * step, step), step)
            for g in range(load.pieces):
                base = buffer[slot, 0, g, at, :].astype(F32)
                for t in range(tenants):
                    sign = buffer[slot, 1 + t, g, at, :].astype(F32)
                    out[g, t, at, :] = (base + scales[t] * sign).astype(BF16)
            return carry

        lax.fori_loop(0, rows // step, combine, 0)
        if i + ahead < len(queue):
            for copy in queue[i + ahead][-1]:
                copy.start()


def load(me, scale, bits, loads, sources, tokens, tenants):
    used = sorted({l.source for l in loads})
    loads = [
        Load(
            used.index(l.source), l.kind, l.scale, l.pieces, l.first, l.ordered, l.by_column, l.shape
        )
        for l in loads
    ]
    far = [x for i in used for x in sources[i]]
    kinds = list(dict.fromkeys((l.pieces,) + l.shape for l in loads))
    scratch = []
    for pieces, rows, columns in kinds:
        scratch.append(pltpu.VMEM((SLOTS, tenants + 1, pieces, rows, columns), BF16))
        scratch.append(pltpu.SemaphoreType.DMA((SLOTS, pieces * (tenants + 1))))
    shapes = [((l.pieces, tenants) + l.shape, BF16) for l in loads] + [((8, LANES), F32)]
    *blocks, token = call(
        functools.partial(load_kernel, bits, loads, len(used), len(tokens), tenants),
        [me, scale],
        tokens,
        shapes,
        far=far,
        scratch=scratch,
        limit=(7 * len(kinds)) * MIB,
    )
    return blocks, token


def weighted(x, block, piece, scales):
    tenants = len(scales)
    draft = x.shape[0] // tenants
    raw = block.shape[1] > tenants
    parts = [
        jnp.dot(
            x[t * draft : (t + 1) * draft], block[piece, raw + t], preferred_element_type=F32
        )
        for t in range(tenants)
    ]
    if not raw:
        return jnp.concatenate(parts, axis=0)
    base = jnp.dot(x, block[piece, 0], preferred_element_type=F32)
    return base + jnp.concatenate([scales[t] * parts[t] for t in range(tenants)], axis=0)


def out_kernel(bits, factor, me_ref, scale_ref, low_ref, high_ref, *rest):
    *w_refs, o_ref, all_ref, x_ref = rest
    half, rows, _ = low_ref.shape
    n = 2 * half
    tenants = w_refs[0].shape[1] - 1
    draft = x_ref.shape[0] // tenants
    me = me_ref[0]
    all_ref[:half] = low_ref[...]
    all_ref[half:] = high_ref[...]
    heads = rows // draft
    for block in range(n):
        where = reversed_bits(block ^ me, bits)
        t, inside = divmod(block, n // tenants)
        for h in range(heads):
            column = (inside * heads + h) * HEAD_SIZE
            x_ref[t * draft : (t + 1) * draft, column : column + HEAD_SIZE] = all_ref[
                where, h * draft : (h + 1) * draft, :
            ]
    base, delta, at = 0.0, [0.0] * tenants, 0
    for w in w_refs:
        deep = w.shape[2]
        x = x_ref[:, at : at + deep]
        base = base + jnp.dot(x, w[0, 0], preferred_element_type=F32)
        for t in range(tenants):
            delta[t] = delta[t] + jnp.dot(
                x[t * draft : (t + 1) * draft], w[0, 1 + t], preferred_element_type=F32
            )
        at += deep
    for t in range(tenants):
        own = slice(t * draft, (t + 1) * draft)
        o_ref[own, :] = (base[own] + scale_ref[t, 0] * factor * delta[t]).astype(BF16)


def out_projection(me, scale, factor, low, high, weights, tokens):
    half, rows, lanes = low.shape
    features = weights[0].shape[-1]
    depth = sum(w.shape[2] for w in weights)
    return call(
        functools.partial(out_kernel, (2 * half).bit_length() - 1, factor),
        [me, scale],
        [low, high] + weights,
        [((tokens, features), BF16)],
        scratch=[pltpu.VMEM((2 * half, rows, lanes), BF16), pltpu.VMEM((tokens, depth), BF16)],
    )[0]


def hidden_kernel(pm_ref, residual_ref, gain_ref, own_ref, got_ref, token_ref, hidden_ref, send_ref):
    tokens = own_ref.shape[0]
    hidden = jnp.dot(pm_ref[...], residual_ref[...], preferred_element_type=F32) + (
        own_ref[...].astype(F32) + got_ref[...].astype(F32)
    )
    hidden_ref[...] = hidden
    scaled = (hidden * gain_ref[...]).astype(BF16)
    pieces = hidden.shape[1] // LANES
    for f in range(pieces):
        send_ref[0, f * tokens : (f + 1) * tokens, :] = scaled[:, f * LANES : (f + 1) * LANES]
    squares = jnp.sum(hidden * hidden, axis=1, keepdims=True)
    send_ref[0, pieces * tokens :, :] = pack_row(to_row(squares))


def hidden_block(pm, residual, gain, own, got, token):
    tokens, features = own.shape
    tall = features // LANES * tokens + STAT_ROWS
    return call(
        hidden_kernel,
        [],
        [pm, residual, gain, own, got, token],
        [((tokens, features), F32), ((1, tall, LANES), BF16)],
    )


def gate_up_kernel(first, last, bits, counts, n_jobs, loads, width, me_ref, *rest):
    n_x = len(counts)
    x_refs, rest = rest[:n_x], rest[n_x + 1 :]
    g_refs, u_refs, rest = rest[:n_jobs], rest[n_jobs : 2 * n_jobs], rest[2 * n_jobs :]
    before = ()
    if not first:
        before, rest = rest[:3], rest[3:]
    if loads:
        w_hbm, s_hbm, *rest = rest
        *rest, sems = rest
        split = 1 if last else 3
        rest, raw_refs = rest[:split], rest[split:]

        def raw_copies(first, rows):
            for i, (load, out) in enumerate(zip(loads, raw_refs)):
                k = 0
                views = load.views(me_ref[0], bits, w_hbm, s_hbm, first, rows)
                for g, (base, signs) in enumerate(views):
                    for j, view in enumerate([base] + signs):
                        to = out.at[g, j, pl.ds(first, rows)]
                        yield pltpu.make_async_copy(view, to, sems.at[i, k])
                        k += 1

        start_halves(raw_copies, loads[0].shape[0])
    tokens = rest[0].shape[0]
    pieces, tenants = g_refs[0].shape[:2]
    draft = tokens // tenants
    columns = (x_refs[0].shape[1] - STAT_ROWS) // tokens
    squares = jnp.zeros((STAT_ROWS, LANES), F32) if first else before[2][...]
    for x_ref, count in zip(x_refs, counts):
        for i in range(count):
            squares = squares + x_ref[i, columns * tokens :, :].astype(F32)
    if last:
        norm = to_column(
            lax.rsqrt(jnp.sum(squares, axis=0, keepdims=True) / width + EPS), tokens
        )
    else:
        rest[2][...] = squares
    for t in range(tenants):
        own = slice(t * draft, (t + 1) * draft)
        sums = [0.0, 0.0] if first else [before[j][own, :] for j in range(2)]
        block = 0
        for x_ref, count in zip(x_refs, counts):
            for i in range(count):
                x = jnp.concatenate(
                    [
                        x_ref[i, f * tokens + t * draft : f * tokens + (t + 1) * draft, :]
                        for f in range(columns)
                    ],
                    axis=1,
                )
                job, piece = divmod(block, pieces)
                block += 1
                for j, refs in enumerate((g_refs, u_refs)):
                    sums[j] = sums[j] + jnp.dot(
                        x, refs[job][piece, t], preferred_element_type=F32
                    )
        if last:
            gate = sums[0] * norm[own]
            up = sums[1] * norm[own]
            rest[0][own, :] = (gate / (1.0 + jnp.exp(-gate)) * up).astype(BF16)
        else:
            rest[0][own, :] = sums[0]
            rest[1][own, :] = sums[1]
    if loads:
        for copy in raw_copies(0, loads[0].shape[0]):
            copy.wait()


def gate_up(me, bits, xs, token, gates, ups, tokens, width, before=(), last=False, loads=(), source=()):
    units = gates[0].shape[-1]
    if last:
        shapes = [((tokens, units), BF16)]
    else:
        shapes = [((tokens, units), F32)] * 2 + [((STAT_ROWS, LANES), F32)]
    scratch = []
    if loads:
        tenants = source[1].shape[0]
        shapes += [((l.pieces, 1 + tenants) + l.shape, BF16) for l in loads]
        scratch = [pltpu.SemaphoreType.DMA((len(loads), loads[0].pieces * (1 + tenants)))]
    counts = tuple(x.shape[0] for x in xs)
    out = call(
        functools.partial(
            gate_up_kernel, not before, last, bits, counts, len(gates), loads, width
        ),
        [me],
        list(xs) + [token] + gates + ups + list(before),
        shapes,
        far=source if loads else (),
        scratch=scratch,
    )
    split = 1 if last else 3
    return out[:split], out[split:]


def down_kernel(factor, n_outs, scale_ref, x_ref, token_ref, *rest):
    w_refs, o_refs = rest[:-n_outs], rest[-n_outs:]
    pieces = w_refs[0].shape[0]
    tenants = scale_ref.shape[0]
    scales = [scale_ref[t, 3] * factor for t in range(tenants)]
    x = x_ref[...]
    per_out = o_refs[0].shape[0]
    for i in range(per_out * n_outs):
        job, piece = divmod(i, pieces)
        total = weighted(x, w_refs[job], piece, scales)
        o_refs[i // per_out][i % per_out] = total.astype(BF16)


def down(scale, factor, active, token, weights, outs):
    features = weights[0].shape[-1]
    tokens = active.shape[0]
    shape = (weights[0].shape[0] * len(weights) // outs, tokens, features)
    return call(
        functools.partial(down_kernel, factor, outs), [scale],
        [active, token] + weights, [(shape, BF16)] * outs,
    )


def add_kernel(keep_ref, got_ref, *outs):
    count = got_ref.shape[0]
    per_out = count // len(outs)
    for i in range(count):
        total = (keep_ref[i].astype(F32) + got_ref[i].astype(F32)).astype(BF16)
        outs[i // per_out][i % per_out] = total


def add(keep, got, outs):
    count, tokens, features = got.shape
    return call(add_kernel, [], [keep, got], [((count // outs, tokens, features), BF16)] * outs)


def finish_kernel(pm_ref, hidden_ref, own_ref, got_ref, o_ref):
    mixed = hidden_ref[...] + (own_ref[0].astype(F32) + got_ref[0].astype(F32))
    o_ref[...] = lax.dot_general(
        pm_ref[...], mixed.astype(BF16), (((0,), (0,)), ((), ())), preferred_element_type=F32
    ).astype(BF16)


def finish(pm, hidden, own, got):
    return call(finish_kernel, [], [pm, hidden, own, got], [(hidden.shape, BF16)], far_out=True)[0]


def layer(
    residual,
    queries,
    draft_token_keys,
    draft_token_values,
    cache_keys,
    cached_value_rows,
    tenant_ids,
    tree_mask,
    cache_lengths,
    out_weight,
    out_signs,
    norm_gain,
    gate_weight,
    up_weight,
    down_weight,
    gate_signs,
    up_signs,
    down_signs,
    delta_scale,
):
    n = lax.axis_size("ctx")
    bits = n.bit_length() - 1
    me = lax.axis_index("ctx").astype(jnp.int32).reshape(1)
    tokens = tenant_ids.shape[0]
    tenants = cache_keys.shape[0]
    features = residual.shape[1]
    all_features, units = gate_weight.shape
    n_kv = lax.axis_size("kv")
    out_factor = (out_weight.shape[0] * n_kv) ** (-0.5)
    unit_factor = all_features ** (-0.5)
    down_factor = (units * n * n_kv) ** (-0.5)
    scale = delta_scale

    def swap(x, bit):
        return lax.ppermute(x, "ctx", [(i, i ^ (1 << bit)) for i in range(n)])

    def swap_kv(x):
        return lax.ppermute(x, "kv", [(i, (i + 1) % n_kv) for i in range(n_kv)])

    sources = [(gate_weight, gate_signs), (up_weight, up_signs), (down_weight, down_signs)]
    pieces = max(1, n // 16)
    eighth, quarter, half = n // 8, n // 4, n // 2
    todo = []
    spans = [(0, 3 * eighth), (half, 7 * eighth), (3 * eighth, half), (7 * eighth, n)]
    for i in [i for a, b in spans for i in range(a, b, pieces)]:
        shape = (features, units)
        todo.append((("gate", i), Load(0, 1, unit_factor, pieces, i, True, False, shape)))
        todo.append((("up", i), Load(1, 2, unit_factor, pieces, i, True, False, shape)))
    downs = [
        (("down", i), Load(2, 3, down_factor, pieces, i, True, True, (units, features)))
        for i in list(range(half, n, pieces)) + list(range(0, half, pieces))
    ]
    n_raw = min(RAW_DOWN, len(downs))
    todo += downs[: len(downs) - n_raw]
    late = downs[len(downs) - n_raw :]
    held = {}

    def fill(count, *tokens_in):
        nonlocal todo
        now, todo = todo[:count], todo[count:]
        if not now:
            return tokens_in[0]
        blocks, token = load(
            me, scale, bits, [l for _, l in now], sources, list(tokens_in), tenants
        )
        for (name, _), block in zip(now, blocks):
            held[name] = block
        return token

    keep, send, pm, residual_here, gain, *out_raw = attention_partials(
        me, cache_lengths, tenant_ids, tree_mask, queries, draft_token_keys, draft_token_values,
        cache_keys, cached_value_rows, residual, norm_gain, out_weight, out_signs, n,
    )
    plan = (PLAN_DOWN + [0] * bits)[: bits - 1]
    for bit in range(bits - 1):
        got = swap(send, bit)
        token = fill(plan[bit], send)
        out = merge(keep, got, token)
        if bit < bits - 2:
            keep, send = out
    (both,) = out
    got = swap(both, bits - 1)
    token = fill(PLAN_TURN, both)
    rows = finish_rows(both, got, token)
    plan = ([0] * bits + PLAN_UP)[-(bits - 2) :]
    for i, bit in enumerate(reversed(range(1, bits - 1))):
        got = swap(rows, bit)
        token = fill(plan[i], rows)
        rows = join(rows, got, token)
    other = swap(rows, 0)
    own = out_projection(me, scale, out_factor, rows, other, out_raw, tokens)

    got = swap_kv(own)
    token = fill(PLAN_LAST[0], own)
    hidden, block = hidden_block(pm, residual_here, gain, own, got, token)
    for bit in reversed(range(3, bits)):
        got = swap(block, bit)
        token = fill(PLAN_LAST[1], block)
        block = join(block, got, token)

    def gate_up_of(xs, spans, token, **options):
        names = [i for a, b in spans for i in range(a, b, pieces)]
        return gate_up(
            me, bits, xs, token, [held["gate", i] for i in names], [held["up", i] for i in names],
            tokens, all_features, **options,
        )

    got_z = swap(block, 2)
    got_x = swap(block, 1)
    got_core = swap(block, 0)
    token = fill(len(todo), block)
    sums, _ = gate_up_of([block], [(0, eighth)], token)
    far_x = swap(got_z, 1)
    got_core_2 = swap(join(got_z, got_x, sums[2]), 0)
    sums, raw = gate_up_of(
        [got_z, got_x, got_core, got_core_2],
        [(eighth, 3 * eighth), (half, 7 * eighth)],
        sums[2],
        before=sums,
        loads=tuple(l for _, l in late),
        source=sources[2],
    )
    for (name, _), array in zip(late, raw):
        held[name] = array
    got_core_3 = swap(far_x, 0)
    sums, _ = gate_up_of([far_x], [(3 * eighth, half)], sums[2], before=sums)
    (active,), _ = gate_up_of(
        [got_core_3], [(7 * eighth, n)], sums[2], before=sums, last=True
    )

    def down_of(a, b, token, outs):
        weights = [held["down", i] for i in range(a, b, pieces)]
        return down(scale, down_factor, active, token, weights, outs)

    send_near, send_far = down_of(half, n, active, 2)
    got_far = swap(send_far, 0)
    got_near = swap(send_near, 0)
    (mine_far,) = down_of(quarter, half, send_near, 1)
    x_late, x_early = add(mine_far, got_far, 2)
    got_early = swap(x_early, 1)
    got_late = swap(x_late, 1)
    (mine_near,) = down_of(0, quarter, x_early, 1)
    keep, send = add(mine_near, got_near, 2)
    (send,) = add(send, got_early, 1)
    got = swap(send, 2)
    (keep,) = add(keep, got_late, 1)
    for bit in range(3, bits):
        keep, send = add(keep, got, 2)
        got = swap(send, bit)
    (total,) = add(keep, got, 1)
    return finish(pm, hidden, total, swap_kv(total))


PLAN_DOWN = [2, 5, 3]
PLAN_TURN = 5
PLAN_UP = [3, 6]
PLAN_LAST = [5, 5]
RAW_DOWN = 8


def solution(mesh):
    return jax.shard_map(
        layer,
        mesh=mesh,
        in_specs=(
            P(None, "ctx"),
            P(None, "kv"),
            P(None, "kv"),
            P(None, "kv"),
            P(None, "ctx", "kv"),
            P(None, "ctx", "kv"),
            P(),
            P(),
            P(),
            P("kv", "ctx"),
            P(None, "kv", "ctx"),
            P("ctx"),
            P(None, ("kv", "ctx")),
            P(None, ("kv", "ctx")),
            P(("kv", "ctx"), None),
            P(None, None, ("kv", "ctx")),
            P(None, None, ("kv", "ctx")),
            P(None, ("kv", "ctx"), None),
            P(),
        ),
        out_specs=P(None, "ctx"),
        check_vma=False,
    )
```

```python
import functools

import jax
import jax.numpy as jnp
from jax import lax
from jax.experimental import pallas as pl
from jax.experimental.pallas import tpu as pltpu
from jax.sharding import PartitionSpec as P

HEAD_SIZE = 128
LANES = 128
STAT_ROWS = 16
NEG = -1e30
EPS = 1e-05
LOG2E = 1.4426950408889634
MIB = 1 << 20
F32 = jnp.float32
BF16 = jnp.bfloat16


IN_VMEM = pl.BlockSpec(memory_space=pltpu.VMEM)
IN_HBM = pl.BlockSpec(memory_space=pl.ANY)


def vmem(x):
    return pltpu.with_memory_space_constraint(x, pltpu.VMEM)


def hbm(x):
    return pltpu.with_memory_space_constraint(x, pltpu.HBM)


def call(kernel, arrays, shapes, far=(), scratch=(), limit=MIB, far_out=False):
    if far_out:
        out_shape = [jax.ShapeDtypeStruct(s, d) for s, d in shapes]
    else:
        out_shape = [pltpu.VMEM(s, d) for s, d in shapes]
    return pl.pallas_call(
        kernel,
        in_specs=[IN_VMEM] * len(arrays) + [IN_HBM] * len(far),
        out_specs=[IN_VMEM] * len(shapes),
        out_shape=out_shape,
        scratch_shapes=list(scratch),
        compiler_params=pltpu.CompilerParams(vmem_limit_bytes=limit),
    )(*[vmem(a) for a in arrays], *[hbm(a) for a in far])


def my_place():
    return lax.axis_index("ctx").astype(jnp.int32)


def scales_of(scale_ref, kind, factor):
    return [scale_ref[t : t + 1, kind : kind + 1] * factor for t in range(scale_ref.shape[0])]


def iota(shape, dim):
    return lax.broadcasted_iota(jnp.int32, shape, dim)


def to_row(column):
    rows = column.shape[0]
    diagonal = iota((rows, LANES), 0) == iota((rows, LANES), 1)
    return jnp.sum(jnp.where(diagonal, column, 0.0), axis=0, keepdims=True)


def to_column(row, rows):
    diagonal = iota((rows, LANES), 0) == iota((rows, LANES), 1)
    return jnp.sum(jnp.where(diagonal, row, 0.0), axis=1, keepdims=True)


def pack_row(row):
    high = row.astype(BF16).astype(F32)
    middle = (row - high).astype(BF16).astype(F32)
    low = row - high - middle
    place = iota((STAT_ROWS, LANES), 0)
    packed = jnp.where(place == 0, high, jnp.where(place == 1, middle, low))
    return jnp.where(place < 3, packed, 0.0).astype(BF16)


def unpack_row(block):
    return jnp.sum(block.astype(F32), axis=0, keepdims=True)


def reversed_bits(value, bits):
    out = 0
    for i in range(bits):
        out = out | (((value >> i) & 1) << (bits - 1 - i))
    return out


def start_halves(copies, rows):
    def half(h, carry):
        for copy in copies(pl.multiple_of(h * (rows // 2), rows // 2), rows // 2):
            copy.start()
        return carry

    lax.fori_loop(0, 2, half, 0)


def attention_kernel(bits, loads, n_sources, *refs):
    me = my_place()
    ids_hbm, tree_hbm, q_hbm, dk_hbm, dv_hbm, k_hbm, v_hbm, len_hbm, res_hbm, gain_hbm = refs[:10]
    sources, refs = refs[10 : 10 + 2 * n_sources], refs[10 + 2 * n_sources :]
    keep_ref, send_ref, pm_ref, res_ref, gain_ref = refs[:5]
    raw_refs, refs = refs[5 : 5 + len(loads)], refs[5 + len(loads) :]
    ids_ref, tree_ref, q_ref, dk_ref, dv_ref, k_ref, v_ref, len_ref, sems, raw_sems = refs
    tenants, slots, _ = k_ref.shape
    small = [
        pltpu.make_async_copy(source, target, sems.at[i])
        for i, (source, target) in enumerate(
            [
                (ids_hbm, ids_ref), (tree_hbm, tree_ref), (q_hbm, q_ref), (dk_hbm, dk_ref),
                (dv_hbm, dv_ref), (len_hbm, len_ref), (res_hbm, res_ref), (gain_hbm, gain_ref),
            ]
        )
    ]
    cache = []
    for t in range(tenants):
        at = len(small) + 2 * t
        cache.append(
            [
                pltpu.make_async_copy(k_hbm.at[t], k_ref.at[t], sems.at[at]),
                pltpu.make_async_copy(v_hbm.at[t], v_ref.at[t], sems.at[at + 1]),
            ]
        )
    raw_copies, raw_rows = raw_copies_of(loads, me, bits, sources, raw_refs, raw_sems)
    for copy in small + [c for pair in cache for c in pair]:
        copy.start()
    start_halves(raw_copies, raw_rows)

    tokens = tree_ref.shape[0]
    draft = tokens // tenants
    groups = dk_ref.shape[1] // HEAD_SIZE
    width = q_ref.shape[1] // dk_ref.shape[1]
    core = me & 1
    rows = keep_ref.shape[1] - STAT_ROWS
    parts = width * draft // rows
    factor = HEAD_SIZE ** (-0.5)
    power = factor * LOG2E
    nt = (((1,), (1,)), ((), ()))

    for copy in small:
        copy.wait()
    a = iota((tokens, tokens), 0)
    b = iota((tokens, tokens), 1)
    across = jnp.broadcast_to(ids_ref[...], (tokens, tokens))
    along = jnp.sum(jnp.where(a == b, across, 0), axis=1, keepdims=True)
    before = (along < across) | ((along == across) & (a < b))
    place = jnp.sum(before.astype(jnp.int32), axis=0, keepdims=True)
    choose = (place == a).astype(F32).astype(BF16)
    pm_ref[...] = choose
    seen_all = jnp.dot(choose, tree_ref[...].astype(F32).astype(BF16), preferred_element_type=F32)
    seen_all = jnp.where(me == 0, seen_all, 0.0)
    mine = jnp.dot(choose, q_ref[...], preferred_element_type=F32).astype(BF16)

    for t in range(tenants):
        seen = jnp.concatenate([seen_all[t * draft : (t + 1) * draft]] * width, axis=0) > 0.5
        live = me * slots + iota((1, slots), 1) < len_ref[t]
        for copy in cache[t]:
            copy.wait()
        for g in range(groups):
            head = slice(g * HEAD_SIZE, (g + 1) * HEAD_SIZE)
            query = jnp.concatenate(
                [
                    mine[
                        t * draft : (t + 1) * draft,
                        (g * width + w) * HEAD_SIZE : (g * width + w + 1) * HEAD_SIZE,
                    ]
                    for w in range(width)
                ],
                axis=0,
            )
            far = lax.dot_general(query, k_ref[t, :, head], nt, preferred_element_type=F32)
            near = lax.dot_general(query, dk_ref[:, head], nt, preferred_element_type=F32)
            far = jnp.where(live, far, NEG)
            near = jnp.where(seen, near, NEG)
            peak = jnp.maximum(
                jnp.max(far, axis=1, keepdims=True), jnp.max(near, axis=1, keepdims=True)
            )
            some = peak > 0.5 * NEG
            far = jnp.exp2((far - peak) * power)
            near = jnp.exp2((near - peak) * power)
            total = jnp.sum(far, axis=1, keepdims=True) + jnp.sum(near, axis=1, keepdims=True)
            value = jnp.dot(far.astype(BF16), v_ref[t, :, head], preferred_element_type=F32)
            value = value + jnp.dot(near.astype(BF16), dv_ref[:, head], preferred_element_type=F32)
            value = value * (1.0 / total)
            level = jnp.where(some, peak * factor + jnp.log(total), NEG)
            for i in range(0, parts, 2):
                even = value[i * rows : (i + 1) * rows]
                odd = value[(i + 1) * rows : (i + 2) * rows]
                even_level = to_row(level[i * rows : (i + 1) * rows])
                odd_level = to_row(level[(i + 1) * rows : (i + 2) * rows])
                block = (t * groups + g) * parts + i
                where = reversed_bits((block >> 1) ^ (me >> 1), bits - 1)
                first = core == 0
                keep_ref[where, :rows, :] = jnp.where(first, even, odd).astype(BF16)
                send_ref[where, :rows, :] = jnp.where(first, odd, even).astype(BF16)
                keep_ref[where, rows:, :] = pack_row(jnp.where(first, even_level, odd_level))
                send_ref[where, rows:, :] = pack_row(jnp.where(first, odd_level, even_level))
    for copy in raw_copies(0, raw_rows):
        copy.wait()


def attention_partials(
    lengths, tenant_ids, tree, queries, dk, dv, keys, values, residual, gain, loads, sources, n
):
    tenants = keys.shape[0]
    tokens = tenant_ids.shape[0]
    groups = dk.shape[1] // HEAD_SIZE
    width = queries.shape[1] // dk.shape[1]
    rows = tokens * groups * width // n
    part = ((n // 2, rows + STAT_ROWS, HEAD_SIZE), BF16)
    gain = gain.reshape(1, gain.shape[0])
    ids = tenant_ids.reshape(1, tokens)
    inner = [ids, tree, queries, dk, dv, keys, values]
    loads, far = used_sources(loads, sources)
    return call(
        functools.partial(attention_kernel, n.bit_length() - 1, loads, len(far) // 2),
        [],
        [part, part, ((tokens, tokens), BF16), (residual.shape, BF16), (gain.shape, F32)]
        + [l.raw_shape(tenants) for l in loads],
        far=inner + [lengths, residual, gain] + far,
        scratch=[pltpu.VMEM(x.shape, x.dtype) for x in inner]
        + [
            pltpu.SMEM(lengths.shape, lengths.dtype),
            pltpu.SemaphoreType.DMA((8 + 2 * tenants,)),
            raw_semaphores(loads, tenants),
        ],
        limit=12 * MIB,
    )


def merged(a_ref, i, b_ref, j, rows):
    a = unpack_row(a_ref[i, rows:, :])
    b = unpack_row(b_ref[j, rows:, :])
    peak = jnp.maximum(a, b)
    ea = jnp.exp(a - peak)
    eb = jnp.exp(b - peak)
    total = ea + eb
    wa = to_column(ea / total, rows)
    mine = a_ref[i, :rows, :].astype(F32)
    value = b_ref[j, :rows, :].astype(F32)
    return (value + (mine - value) * wa).astype(BF16), peak + jnp.log(total)


def merge_kernel(keep_ref, got_ref, token_ref, *outs):
    count = got_ref.shape[0]
    rows = keep_ref.shape[1] - STAT_ROWS
    for i in range(count):
        value, level = merged(keep_ref, i, got_ref, i, rows)
        per_out = count // len(outs)
        out, j = outs[i // per_out], i % per_out
        out[j, :rows, :] = value
        out[j, rows:, :] = pack_row(level)


def merge(keep, got, token):
    count, tall, lanes = got.shape
    outs = 1 if count == 2 else 2
    shapes = [((count // outs, tall, lanes), BF16)] * outs
    return call(merge_kernel, [keep, got, token], shapes)


def finish_rows_kernel(own_ref, got_ref, token_ref, o_ref):
    rows = o_ref.shape[1]
    for i in range(2):
        o_ref[i] = merged(own_ref, i, got_ref, 1 - i, rows)[0]


def finish_rows(own, got, token):
    _, tall, lanes = own.shape
    return call(
        finish_rows_kernel, [own, got, token],
        [((2, tall - STAT_ROWS, lanes), BF16)],
    )[0]


def join_kernel(a_ref, b_ref, token_ref, o_ref):
    count = a_ref.shape[0]
    o_ref[:count] = a_ref[...]
    o_ref[count:] = b_ref[...]


def join(a, b, token):
    shape = (a.shape[0] + b.shape[0],) + a.shape[1:]
    return call(join_kernel, [a, b, token], [(shape, a.dtype)])[0]


class Load:
    def __init__(self, source, kind, scale, pieces, block_of, by_column, shape):
        self.source, self.kind, self.scale, self.pieces = source, kind, scale, pieces
        self.block_of, self.by_column, self.shape = block_of, by_column, shape

    def at(self, source):
        return Load(
            source, self.kind, self.scale, self.pieces, self.block_of, self.by_column, self.shape
        )

    def raw_shape(self, tenants):
        return ((self.pieces, 1 + tenants) + self.shape, BF16)

    def views(self, me, bits, w, s, first, count):
        rows, columns = self.shape
        for g in range(self.pieces):
            block = self.block_of(g, me, bits)
            if self.by_column:
                at = (
                    pl.ds(first, count),
                    pl.ds(pl.multiple_of(block * columns, columns), columns),
                )
            else:
                at = (pl.ds(pl.multiple_of(block * rows, rows) + first, count),)
            yield w.at[at], [s.at[(t,) + at] for t in range(s.shape[0])]


def in_order(start):
    return lambda g, me, bits: reversed_bits(start + g, bits) ^ me


def own_core_first(start, count):
    def block_of(g, me, bits):
        i, core = start + g, me & 1
        return 2 * i + core if i < count // 2 else 2 * i - count + 1 - core

    return block_of


def used_sources(loads, sources):
    used = sorted({l.source for l in loads})
    return [l.at(used.index(l.source)) for l in loads], [x for i in used for x in sources[i]]


def raw_semaphores(loads, tenants):
    return pltpu.SemaphoreType.DMA((len(loads), max(l.pieces for l in loads) * (1 + tenants)))


def raw_copies_of(loads, me, bits, sources, outs, sems):
    whole = min(l.shape[0] for l in loads)

    def copies(first, count):
        for i, (load, out) in enumerate(zip(loads, outs)):
            many = load.shape[0] // whole
            w, s = sources[2 * load.source], sources[2 * load.source + 1]
            k = 0
            views = load.views(me, bits, w, s, first * many, count * many)
            for g, (base, signs) in enumerate(views):
                for j, view in enumerate([base] + signs):
                    to = out.at[g, j, pl.ds(first * many, count * many)]
                    yield pltpu.make_async_copy(view, to, sems.at[i, k])
                    k += 1

    return copies, whole


def groups_of(folds):
    groups = []
    for load in folds:
        if load.kind == 2:
            groups[-1].append(load)
        else:
            groups.append([load])
    return groups


def place_of(folds, i):
    for group, loads in enumerate(groups_of(folds)):
        if i < len(loads):
            return group, i * loads[0].pieces
        i -= len(loads)


def load_kernel(bits, loads, folds, n_sources, n_tokens, tenants, scale_ref, *refs):
    refs = refs[n_tokens:]
    raw_refs, refs = refs[: len(folds)], refs[len(folds) :]
    sources, refs = refs[: 2 * n_sources], refs[2 * n_sources :]
    n_outs = len(groups_of(folds))
    outs, refs = refs[:n_outs], refs[n_outs:]
    new_refs, token_ref, sems = refs[: len(loads)], refs[len(loads)], refs[len(loads) + 1 :]
    token_ref[...] = jnp.zeros_like(token_ref)
    if loads:
        copies, rows = raw_copies_of(loads, my_place(), bits, sources, new_refs, sems[0])
        start_halves(copies, rows)
    for i, (load, raw) in enumerate(zip(folds, raw_refs)):
        group, first = place_of(folds, i)
        out = outs[group].at[pl.ds(first, load.pieces)]
        rows = load.shape[0]
        step = min(64, rows)
        scales = scales_of(scale_ref, load.kind, load.scale)
        scales = [jnp.broadcast_to(x, (step, load.shape[1])) for x in scales]

        def fold(k, carry, out=out, raw=raw, scales=scales, load=load, step=step):
            at = pl.ds(pl.multiple_of(k * step, step), step)
            for g in range(load.pieces):
                base = raw[g, 0, at, :].astype(F32)
                for t in range(tenants):
                    sign = raw[g, 1 + t, at, :].astype(F32)
                    out[g, t, at, :] = (base + scales[t] * sign).astype(BF16)
            return carry

        lax.fori_loop(0, rows // step, fold, 0)
    if loads:
        for copy in copies(0, min(l.shape[0] for l in loads)):
            copy.wait()


def load(scale, bits, loads, folds, raws, sources, tokens, tenants):
    loads, far = used_sources(loads, sources)
    groups = groups_of(folds)
    shapes = [
        ((sum(l.pieces for l in group), tenants) + group[0].shape, BF16) for group in groups
    ] + [l.raw_shape(tenants) for l in loads]
    *blocks, token = call(
        functools.partial(
            load_kernel, bits, loads, folds, len(far) // 2, len(tokens), tenants
        ),
        [scale] + tokens + raws,
        shapes + [((8, LANES), F32)],
        far=far,
        scratch=[raw_semaphores(loads, tenants)] if loads else [],
        limit=MIB,
    )
    return blocks[: len(groups)], blocks[len(groups) :], token


def weighted(x, block, piece, scales):
    tenants = len(scales)
    draft = x.shape[0] // tenants
    raw = block.shape[1] > tenants
    parts = [
        jnp.dot(
            x[t * draft : (t + 1) * draft], block[piece, raw + t], preferred_element_type=F32
        )
        for t in range(tenants)
    ]
    if not raw:
        return jnp.concatenate(parts, axis=0)
    base = jnp.dot(x, block[piece, 0], preferred_element_type=F32)
    return base + jnp.concatenate([scales[t] * parts[t] for t in range(tenants)], axis=0)


def out_kernel(
    bits, factor, last, n_jobs, loads, n_sources, scale_ref, rows_ref, *rest
):
    w_refs, rest = rest[:n_jobs], rest[n_jobs:]
    if last:
        before_ref, *rest = rest
    sources, rest = rest[: 2 * n_sources], rest[2 * n_sources :]
    o_ref, raw_refs, x_ref = rest[0], rest[1 : 1 + len(loads)], rest[1 + len(loads)]
    if loads:
        raw_copies, raw_rows = raw_copies_of(loads, my_place(), bits, sources, raw_refs, rest[-1])
        start_halves(raw_copies, raw_rows)
    half, _, _ = rows_ref.shape
    pieces, deep = w_refs[0].shape[0], w_refs[0].shape[2]
    tenants = scale_ref.shape[0]
    draft = o_ref.shape[0] // tenants
    me = my_place()
    scales = scales_of(scale_ref, 0, factor)
    chunks = 2 * half // tenants
    block_of = own_core_first(chunks // 2 if last else 0, chunks)
    for i in range(chunks // 2):
        for t in range(tenants):
            where = reversed_bits((t * chunks + block_of(i, me, bits)) ^ me, bits) & (half - 1)
            for h in range(deep // HEAD_SIZE):
                column = i * deep + h * HEAD_SIZE
                x_ref[t * draft : (t + 1) * draft, column : column + HEAD_SIZE] = rows_ref[
                    where, h * draft : (h + 1) * draft, :
                ]
    base, delta = 0.0, [0.0] * tenants
    for i in range(chunks // 2):
        job, piece = divmod(i, pieces)
        x = x_ref[:, i * deep : (i + 1) * deep]
        base = base + jnp.dot(x, w_refs[job][piece, 0], preferred_element_type=F32)
        for t in range(tenants):
            delta[t] = delta[t] + jnp.dot(
                x[t * draft : (t + 1) * draft], w_refs[job][piece, 1 + t],
                preferred_element_type=F32,
            )
    for t in range(tenants):
        own = slice(t * draft, (t + 1) * draft)
        total = base[own] + scales[t] * delta[t]
        if last:
            total = (total + before_ref[own, :]).astype(BF16)
        o_ref[own, :] = total
    if loads:
        for copy in raw_copies(0, raw_rows):
            copy.wait()


def out_projection(scale, factor, rows, weights, tokens, loads, sources, before=()):
    half = rows.shape[0]
    features = weights[0].shape[-1]
    depth = sum(w.shape[0] * w.shape[2] for w in weights)
    last = len(before) > 0
    tenants = scale.shape[0]
    loads, far = used_sources(loads, sources)
    own, *raw = call(
        functools.partial(
            out_kernel, (2 * half).bit_length() - 1, factor, last, len(weights), loads,
            len(far) // 2,
        ),
        [scale, rows] + weights + list(before),
        [((tokens, features), BF16 if last else F32)] + [l.raw_shape(tenants) for l in loads],
        far=far,
        scratch=[pltpu.VMEM((tokens, depth), BF16)]
        + ([raw_semaphores(loads, tenants)] if loads else []),
    )
    return own, raw


def hidden_kernel(pm_ref, residual_ref, gain_ref, own_ref, got_ref, token_ref, hidden_ref, send_ref):
    tokens = own_ref.shape[0]
    hidden = jnp.dot(pm_ref[...], residual_ref[...], preferred_element_type=F32) + (
        own_ref[...].astype(F32) + got_ref[...].astype(F32)
    )
    hidden_ref[...] = hidden
    scaled = (hidden * gain_ref[...]).astype(BF16)
    pieces = hidden.shape[1] // LANES
    for f in range(pieces):
        send_ref[0, f * tokens : (f + 1) * tokens, :] = scaled[:, f * LANES : (f + 1) * LANES]
    squares = jnp.sum(hidden * hidden, axis=1, keepdims=True)
    send_ref[0, pieces * tokens :, :] = pack_row(to_row(squares))


def hidden_block(pm, residual, gain, own, got, token):
    tokens, features = own.shape
    tall = features // LANES * tokens + STAT_ROWS
    return call(
        hidden_kernel,
        [pm, residual, gain, own, got, token],
        [((tokens, features), F32), ((1, tall, LANES), BF16)],
    )


def gate_up_kernel(
    first, last, bits, counts, n_jobs, loads, width, n_down, factor, scale_ref, *rest
):
    n_x = len(counts)
    x_refs, rest = rest[:n_x], rest[n_x + 1 :]
    pair_refs, rest = rest[:n_jobs], rest[n_jobs:]
    before = ()
    if not first:
        before, rest = rest[:3], rest[3:]
    down_refs, rest = rest[:n_down], rest[n_down:]
    if loads:
        w_hbm, s_hbm, *rest = rest
        *rest, sems = rest
        split = 3
        rest, raw_refs = rest[:split], rest[split:]

        raw_copies, raw_rows = raw_copies_of(
            loads, my_place(), bits, (w_hbm, s_hbm), raw_refs, sems
        )
        start_halves(raw_copies, raw_rows)
    tokens = rest[0].shape[0]
    pieces, tenants = pair_refs[0].shape[0] // 2, pair_refs[0].shape[1]
    draft = tokens // tenants
    columns = (x_refs[0].shape[1] - STAT_ROWS) // tokens
    squares = jnp.zeros((STAT_ROWS, LANES), F32) if first else before[2][...]
    for x_ref, count in zip(x_refs, counts):
        for i in range(count):
            squares = squares + x_ref[i, columns * tokens :, :].astype(F32)
    if last:
        norm = to_column(
            lax.rsqrt(jnp.sum(squares, axis=0, keepdims=True) / width + EPS), tokens
        )
    else:
        rest[2][...] = squares
    for t in range(tenants):
        own = slice(t * draft, (t + 1) * draft)
        sums = [0.0, 0.0] if first else [before[j][own, :] for j in range(2)]
        block = 0
        for x_ref, count in zip(x_refs, counts):
            for i in range(count):
                x = jnp.concatenate(
                    [
                        x_ref[i, f * tokens + t * draft : f * tokens + (t + 1) * draft, :]
                        for f in range(columns)
                    ],
                    axis=1,
                )
                job, piece = divmod(block, pieces)
                block += 1
                for j in range(2):
                    sums[j] = sums[j] + jnp.dot(
                        x, pair_refs[job][j * pieces + piece, t], preferred_element_type=F32
                    )
        if last:
            gate = sums[0] * norm[own]
            up = sums[1] * norm[own]
            rest[0][own, :] = (gate / (1.0 + jnp.exp(-gate)) * up).astype(BF16)
        else:
            rest[0][own, :] = sums[0]
            rest[1][own, :] = sums[1]
    if last:
        down_products(factor, scale_ref, rest[0][...], down_refs, rest[1:3])
    if loads:
        for copy in raw_copies(0, raw_rows):
            copy.wait()


def gate_up(
    scale, bits, xs, token, pairs, tokens, width, before=(), downs=(), factor=1.0,
    loads=(), source=(),
):
    units = pairs[0].shape[-1]
    last = len(downs) > 0
    if last:
        shape = (downs[0].shape[0] * len(downs) // 2, tokens, downs[0].shape[-1])
        shapes = [((tokens, units), BF16)] + [(shape, BF16)] * 2
    else:
        shapes = [((tokens, units), F32)] * 2 + [((STAT_ROWS, LANES), F32)]
    scratch = []
    if loads:
        tenants = source[1].shape[0]
        loads = tuple(l.at(0) for l in loads)
        shapes += [l.raw_shape(tenants) for l in loads]
        scratch = [raw_semaphores(loads, tenants)]
    counts = tuple(x.shape[0] for x in xs)
    out = call(
        functools.partial(
            gate_up_kernel, not before, last, bits, counts, len(pairs), loads, width, len(downs),
            factor,
        ),
        [scale] + list(xs) + [token] + pairs + list(before) + list(downs),
        shapes,
        far=source if loads else (),
        scratch=scratch,
    )
    return out[:3], out[3:]


def down_products(factor, scale_ref, x, w_refs, o_refs):
    pieces = w_refs[0].shape[0]
    scales = scales_of(scale_ref, 3, factor)
    per_out = o_refs[0].shape[0]
    for i in range(per_out * len(o_refs)):
        job, piece = divmod(i, pieces)
        total = weighted(x, w_refs[job], piece, scales)
        o_refs[i // per_out][i % per_out] = total.astype(BF16)


def down_kernel(factor, scale_ref, x_ref, token_ref, *rest):
    down_products(factor, scale_ref, x_ref[...], rest[:-1], rest[-1:])


def down(scale, factor, active, token, weights):
    features = weights[0].shape[-1]
    tokens = active.shape[0]
    shape = (weights[0].shape[0] * len(weights), tokens, features)
    return call(
        functools.partial(down_kernel, factor), [scale, active, token] + weights, [(shape, BF16)]
    )[0]


def add_kernel(keep_ref, got_ref, *outs):
    count = got_ref.shape[0]
    per_out = count // len(outs)
    for i in range(count):
        total = (keep_ref[i].astype(F32) + got_ref[i].astype(F32)).astype(BF16)
        outs[i // per_out][i % per_out] = total


def total_kernel(*refs):
    *parts, o_ref = refs
    total = parts[0][...].astype(F32)
    for part in parts[1:]:
        total = total + part[...].astype(F32)
    o_ref[...] = total.astype(BF16)


def total_of(parts):
    return call(total_kernel, parts, [(parts[0].shape, BF16)])[0]


def add(keep, got, outs):
    count, tokens, features = got.shape
    return call(add_kernel, [keep, got], [((count // outs, tokens, features), BF16)] * outs)


def finish_kernel(pm_ref, hidden_ref, own_ref, got_ref, o_ref):
    mixed = hidden_ref[...] + (own_ref[0].astype(F32) + got_ref[0].astype(F32))
    o_ref[...] = lax.dot_general(
        pm_ref[...], mixed.astype(BF16), (((0,), (0,)), ((), ())), preferred_element_type=F32
    ).astype(BF16)


def finish(pm, hidden, own, got):
    return call(finish_kernel, [pm, hidden, own, got], [(hidden.shape, BF16)], far_out=True)[0]


def layer(
    residual,
    queries,
    draft_token_keys,
    draft_token_values,
    cache_keys,
    cached_value_rows,
    tenant_ids,
    tree_mask,
    cache_lengths,
    out_weight,
    out_signs,
    norm_gain,
    gate_weight,
    up_weight,
    down_weight,
    gate_signs,
    up_signs,
    down_signs,
    delta_scale,
):
    n = lax.axis_size("ctx")
    bits = n.bit_length() - 1
    tokens = tenant_ids.shape[0]
    tenants = cache_keys.shape[0]
    features = residual.shape[1]
    all_features, units = gate_weight.shape
    n_kv = lax.axis_size("kv")
    out_factor = (out_weight.shape[0] * n_kv) ** (-0.5)
    unit_factor = all_features ** (-0.5)
    down_factor = (units * n * n_kv) ** (-0.5)
    scale = delta_scale

    def swap(x, bit):
        return lax.ppermute(x, "ctx", [(i, i ^ (1 << bit)) for i in range(n)])

    def swap_kv(x):
        return lax.ppermute(x, "kv", [(i, (i + 1) % n_kv) for i in range(n_kv)])

    sources = [
        (gate_weight, gate_signs),
        (up_weight, up_signs),
        (down_weight, down_signs),
        (out_weight, out_signs),
    ]
    pieces = max(1, n // 16)
    eighth, quarter, half = n // 8, n // 4, n // 2
    todo = []
    spans = [(0, 3 * eighth), (half, 7 * eighth), (3 * eighth, half), (7 * eighth, n)]
    for i in [i for a, b in spans for i in range(a, b, pieces)]:
        shape = (features, units)
        at = in_order(i)
        todo.append((("gate", i), Load(0, 1, unit_factor, pieces, at, False, shape)))
        todo.append((("up", i), Load(1, 2, unit_factor, pieces, at, False, shape)))
    downs = [
        (("down", i), Load(2, 3, down_factor, pieces, in_order(i), True, (units, features)))
        for i in list(range(half, n, pieces)) + list(range(quarter, half, pieces))
        + list(range(0, quarter, pieces))
    ]
    todo += downs[:DOWN_EARLY]
    late, latest = downs[DOWN_EARLY:DOWN_LATE], downs[DOWN_LATE:]
    chunks = n // tenants
    outs = [
        Load(
            3, 0, out_factor, pieces, own_core_first(i, chunks), False,
            (out_weight.shape[0] // chunks, features),
        )
        for i in range(0, chunks, pieces)
    ]
    held, pending = {}, []

    def take(count):
        nonlocal todo
        now, todo = todo[:count], todo[count:]
        return now

    def keep_raw(now, raw):
        pending.extend(now)
        for (name, _), block in zip(now, raw):
            held[name] = block

    def fill(plan, *tokens_in):
        count, folds = plan
        now = take(count)
        old = pending[:folds]
        del pending[:folds]
        if not now and not old:
            return tokens_in[0]
        folded, raw, token = load(
            scale, bits, [l for _, l in now], [l for _, l in old],
            [held[name] for name, _ in old], sources, list(tokens_in), tenants,
        )
        firsts = [name for name, l in old if l.kind != 2]
        for name, block in zip(firsts, folded):
            held[name] = block
        keep_raw(now, raw)
        return token

    early = take(EARLY)
    keep, send, pm, residual_here, gain, *raw = attention_partials(
        cache_lengths, tenant_ids, tree_mask, queries, draft_token_keys, draft_token_values,
        cache_keys, cached_value_rows, residual, norm_gain, outs + [l for _, l in early],
        sources, n,
    )
    out_raw = raw[: len(outs)]
    keep_raw(early, raw[len(outs) :])
    plan = (PLAN_DOWN + [(0, 0)] * bits)[: bits - 1]
    for bit in range(bits - 1):
        got = swap(send, bit)
        token = fill(plan[bit], send)
        out = merge(keep, got, token)
        if bit < bits - 2:
            keep, send = out
    (both,) = out
    got = swap(both, bits - 1)
    token = fill(PLAN_TURN, both)
    rows = finish_rows(both, got, token)
    plan = ([(0, 0)] * bits + PLAN_UP)[-(bits - 2) :]
    for i, bit in enumerate(reversed(range(1, bits - 1))):
        got = swap(rows, bit)
        token = fill(plan[i], rows)
        rows = join(rows, got, token)
    other = swap(rows, 0)
    split = len(out_raw) // 2
    now = take(PLAN_OUT[0])
    own, raw = out_projection(
        scale, out_factor, rows, out_raw[:split], tokens, [l for _, l in now], sources
    )
    keep_raw(now, raw)
    now = take(PLAN_OUT[1])
    own, raw = out_projection(
        scale, out_factor, other, out_raw[split:], tokens, [l for _, l in now], sources,
        [own],
    )
    keep_raw(now, raw)

    got = swap_kv(own)
    token = fill(PLAN_LAST[0], own)
    hidden, block = hidden_block(pm, residual_here, gain, own, got, token)
    for bit in reversed(range(3, bits)):
        got = swap(block, bit)
        token = fill(PLAN_LAST[1], block)
        block = join(block, got, token)

    def gate_up_of(xs, spans, token, **options):
        names = [i for a, b in spans for i in range(a, b, pieces)]
        return gate_up(
            scale, bits, xs, token, [held["gate", i] for i in names],
            tokens, all_features, **options,
        )

    got_z = swap(block, 2)
    got_x = swap(block, 1)
    got_core = swap(block, 0)
    token = fill((len(todo), PLAN_LAST[2]), block)
    sums, _ = gate_up_of([block], [(0, eighth)], token)
    far_x = swap(got_z, 1)
    got_core_2 = swap(join(got_z, got_x, sums[2]), 0)
    sums, raw = gate_up_of(
        [got_z, got_x, got_core, got_core_2],
        [(eighth, 3 * eighth), (half, 7 * eighth)],
        sums[2],
        before=sums,
        loads=tuple(l for _, l in late),
        source=sources[2],
    )
    for (name, _), array in zip(late, raw):
        held[name] = array
    got_core_3 = swap(far_x, 0)
    sums, _ = gate_up_of([far_x], [(3 * eighth, half)], sums[2], before=sums)
    (active, send_near, send_far), raw = gate_up_of(
        [got_core_3],
        [(7 * eighth, n)],
        sums[2],
        before=sums,
        downs=[held["down", i] for i in range(half, n, pieces)],
        factor=down_factor,
        loads=tuple(l for _, l in latest),
        source=sources[2],
    )
    for (name, _), array in zip(latest, raw):
        held[name] = array

    def down_of(a, b, token):
        weights = [held["down", i] for i in range(a, b, pieces)]
        return down(scale, down_factor, active, token, weights)

    def swap_position(x, position):
        mask = reversed_bits(position, bits)
        return lax.ppermute(x, "ctx", [(i, i ^ mask) for i in range(n)])

    got_far = swap(send_far, 0)
    got_near = swap(send_near, 0)
    mine_far = down_of(quarter, half, send_near)
    x_late, x_early = add(mine_far, got_far, 2)
    got_early = swap(x_early, 1)
    got_late = swap(x_late, 1)
    mine_near = down_of(0, quarter, x_early)
    late_part, early_part = add(mine_near, got_near, 2)
    early_parts = add(early_part, got_early, eighth)
    arrived = [swap_position(x, eighth + i) for i, x in reversed(list(enumerate(early_parts)))]
    own, *late_parts = add(late_part, got_late, eighth)
    arrived += [swap_position(x, 1 + i) for i, x in reversed(list(enumerate(late_parts)))]
    total = total_of([own] + arrived)
    return finish(pm, hidden, total, swap_kv(total))


EARLY = 2
DOWN_EARLY = 8
DOWN_LATE = 12
PLAN_DOWN = [(0, 2), (7, 0), (3, 6)]
PLAN_TURN = (4, 4)
PLAN_UP = [(5, 4), (6, 4)]
PLAN_OUT = (0, 0)
PLAN_LAST = [(3, 6), (4, 4), 4]


def solution(mesh):
    return jax.shard_map(
        layer,
        mesh=mesh,
        in_specs=(
            P(None, "ctx"),
            P(None, "kv"),
            P(None, "kv"),
            P(None, "kv"),
            P(None, "ctx", "kv"),
            P(None, "ctx", "kv"),
            P(),
            P(),
            P(),
            P("kv", "ctx"),
            P(None, "kv", "ctx"),
            P("ctx"),
            P(None, ("kv", "ctx")),
            P(None, ("kv", "ctx")),
            P(("kv", "ctx"), None),
            P(None, None, ("kv", "ctx")),
            P(None, None, ("kv", "ctx")),
            P(None, ("kv", "ctx"), None),
            P(),
        ),
        out_specs=P(None, "ctx"),
        check_vma=False,
    )
```
